512 devices in a mesh: dp: 64 (over z, y_hi, core), ctx: 8 (over y_lo, x).
Axes of the slice: x: 4, y: 8 (y_hi: 4, y_lo: 2; y = y_hi * 2 + y_lo), z: 8, core: 2. Of those that a mesh axis runs over, the one named last changes fastest.
Arguments:
- glu_in: bfloat16 [64, 1024, 1536], P('dp', 'ctx'), may hold values from -40 to 40
- lengths: int32 [64], P('dp'), may hold values from 512 to 1024, as said below
- kernel: float32 [31, 768], replicated, may hold values from -1 to 1
- bn_gain: float32 [768], replicated, may hold values from 0.1 to 1.9
- bn_bias: float32 [768], replicated, may hold values from -1 to 1
- proj_weight: bfloat16 [768, 768], P('dp'), may hold values from -0.21875 to 0.21875
- cotangent: bfloat16 [64, 1024, 768], P('dp', 'ctx'), may hold values from -6 to 6
Outputs:
- out: bfloat16 [64, 1024, 768], P('dp', 'ctx')
- grad_glu_in: bfloat16 [64, 1024, 1536], P('dp', 'ctx')
- grad_proj: float32 [768, 768], P('dp')
- grad_kernel: float32 [31, 768], replicated
- grad_gain: float32 [768], replicated
- grad_bias: float32 [768], replicated
The draws below stay inside these ranges and needn't reach their ends.
Inputs may be any that keep to these rules, and one draw needn't show every extreme that they name: `lengths`: positions below a sequence's length are real tokens and the rest padding; some sequence is full and some has exactly 512 valid positions.
All inputs are finite; a program needn't handle non-finite values.
Results may differ from the reference program's by a relative error of at most 0.013.
Values may be sent and summed in bfloat16 or wider, within the bound.
A program may use at most 64 MiB of HBM per device.

```python
import jax
import jax.numpy as jnp
from jax import lax

C = 768
DOUT = 768
K = 31
SEQS = 64
LEN = 1024


def draw_glu_in(key, part):
    key_base = jax.random.fold_in(key, 11)
    key_offset = jax.random.fold_in(key, 12)
    seq_pos = jnp.arange(SEQS, dtype=jnp.float32)[:, None, None] / (SEQS - 1)
    tok_pos = jnp.arange(LEN, dtype=jnp.float32)[None, :, None] / (LEN - 1)
    rising = jnp.exp(0.55 * (seq_pos + tok_pos))
    base = jax.random.normal(key_base, (SEQS, LEN, 2 * C), jnp.float32)
    offset = jax.random.uniform(key_offset, (1, 1, C), jnp.float32, 0.2, 0.8)
    value = (base[:, :, :C] + offset) * rising
    gate = base[:, :, C:] * 1.5
    return jnp.concatenate([value, gate], 2).astype(jnp.bfloat16)


def draw_lengths(key, part):
    key_raw = jax.random.fold_in(key, 21)
    key_order = jax.random.fold_in(key, 22)
    raw = LEN - jax.random.randint(key_raw, (SEQS,), 0, LEN // 2 + 1)
    order = jax.random.permutation(key_order, SEQS)
    slots = jnp.arange(SEQS)
    raw = jnp.where(slots == order[0], LEN, raw)
    raw = jnp.where(slots == order[1], LEN // 2, raw)
    return raw.astype(jnp.int32)


def steps_of(key, shape, split, least, high):
    gain, own = 1.0, jax.random.fold_in(key, 6)
    for dim, blocks in split:
        steps = jnp.exp(jax.random.uniform(jax.random.fold_in(own, dim), (blocks,), jnp.float32, least / len(split), high / len(split)))
        gain = gain * jnp.repeat(steps, shape[dim] // blocks).reshape([-1 if axis == dim else 1 for axis in range(len(shape))])
    return gain


def noise(key, dims, spread, most, pieces=(), held_as=jnp.bfloat16):
    array = jax.random.normal(key, dims, jnp.float32) * spread
    if len(pieces) > 0:
        array = steps_of(key, dims, pieces, -0.22, 0.18) * array
    return jnp.clip(array, min=-most, max=most).astype(held_as)


def setup_inputs(seed: int = 0) -> dict:
    arg_keys = jax.random.split(jax.random.key(seed), 8)
    return {
        "glu_in": draw_glu_in(jax.random.fold_in(arg_keys[7], 71), 0),
        "lengths": draw_lengths(jax.random.fold_in(arg_keys[7], 71), 0),
        "kernel": noise(arg_keys[2], (K, C), K ** -0.5, 1.0, (), jnp.float32),
        "bn_gain": jnp.clip(1.0 + 0.18 * jax.random.normal(arg_keys[3], (C,), jnp.float32), 0.1, 1.9),
        "bn_bias": jnp.clip(jax.random.uniform(arg_keys[4], (C,), jnp.float32, -1.0, 1.0), -1.0, 1.0),
        "proj_weight": noise(arg_keys[5], (C, DOUT), C ** -0.5, 0.21875, ((0, 64),)),
        "cotangent": noise(arg_keys[6], (SEQS, LEN, DOUT), 1.0, 6.0, ((0, 64), (1, 8))),
    }


eps = 1e-05

def prepare(glu_row, length):
    value = glu_row[:, :C].astype(jnp.float32)
    gate = glu_row[:, C:].astype(jnp.float32)
    live = (jnp.arange(LEN, dtype=jnp.int32) < length).astype(jnp.float32)[:, None]
    sig_gate = jax.nn.sigmoid(gate)
    unit_out = (live * value * sig_gate).astype(jnp.bfloat16)
    return (value, sig_gate, live, unit_out)

def shifted_sum(padded, kernel, flip):
    total = jnp.zeros((LEN, C), jnp.float32)
    for shift_k in range(K):
        first = K - 1 - shift_k if flip else shift_k
        total = total + kernel[shift_k] * padded[first:first + LEN]
    return total

def reference(glu_in, lengths, kernel, bn_gain, bn_bias, proj_weight, cotangent):
    reach = (K - 1) // 2

    def conv_of(glu_row, length):
        value, sig_gate, live, unit_out = prepare(glu_row, length)
        padded = jnp.pad(unit_out.astype(jnp.float32), ((reach, reach), (0, 0)))
        return (value, sig_gate, live, padded, shifted_sum(padded, kernel, False))

    def first_pass(carry, xs):
        parts = conv_of(xs[0], xs[1])
        live, conv = (parts[2], parts[4])
        return ((carry[0] + lax.optimization_barrier(jnp.sum(live * conv, 0)), carry[1] + jnp.sum(live)), None)
    start = (jnp.zeros((C,), jnp.float32), jnp.zeros((), jnp.float32))
    (total_z, count), _ = lax.scan(first_pass, start, (glu_in, lengths))
    mean = total_z / count

    def second_pass(carry, xs):
        parts = conv_of(xs[0], xs[1])
        centered = parts[4] - mean
        return (carry + lax.optimization_barrier(jnp.sum(parts[2] * centered * centered, 0)), None)
    var_sum, _ = lax.scan(second_pass, jnp.zeros((C,), jnp.float32), (glu_in, lengths))
    inv_std = lax.rsqrt(var_sum / count + eps)

    def norm_of(glu_row, length):
        value, sig_gate, live, padded, conv = conv_of(glu_row, length)
        normed = (conv - mean) * inv_std
        pre = bn_gain * normed + bn_bias
        sig_pre = jax.nn.sigmoid(pre)
        act = (live * pre * sig_pre).astype(jnp.bfloat16)
        return (value, sig_gate, live, padded, normed, pre, sig_pre, act)

    def third_pass(carry, xs):
        parts = norm_of(xs[0], xs[1])
        live, normed, pre, sig_pre, act = (parts[2], parts[4], parts[5], parts[6], parts[7])
        out_row = jnp.dot(act, proj_weight, preferred_element_type=jnp.float32).astype(jnp.bfloat16)
        d_act = jnp.dot(xs[2], proj_weight.T, preferred_element_type=jnp.float32)
        d_pre = live * d_act * sig_pre * (1.0 + pre * (1.0 - sig_pre))
        grad_sum = carry[0] + jnp.dot(act.T, xs[2], preferred_element_type=jnp.float32)
        return ((grad_sum, carry[1] + lax.optimization_barrier(jnp.sum(d_pre, 0)), carry[2] + lax.optimization_barrier(jnp.sum(d_pre * normed, 0))), (out_row, d_pre))
    start = (jnp.zeros((C, DOUT), jnp.float32), jnp.zeros((C,), jnp.float32), jnp.zeros((C,), jnp.float32))
    (proj_sum, sum_bias, sum_gain), (out, d_pres) = lax.scan(third_pass, start, (glu_in, lengths, cotangent))

    def fourth_pass(carry, xs):
        parts = norm_of(xs[0], xs[1])
        value, sig_gate, live, padded, normed = (parts[0], parts[1], parts[2], parts[3], parts[4])
        d_pre = xs[2]
        d_conv = (live * bn_gain * inv_std * (d_pre - sum_bias / count - normed * sum_gain / count)).astype(jnp.bfloat16)
        d_wide = d_conv.astype(jnp.float32)
        terms = jnp.stack([lax.optimization_barrier(jnp.sum(d_wide * padded[shift_k:shift_k + LEN], 0)) for shift_k in range(K)])
        d_padded = jnp.pad(d_wide, ((reach, reach), (0, 0)))
        d_unit = live * shifted_sum(d_padded, kernel, True)
        grad_row = jnp.concatenate([d_unit * sig_gate, d_unit * value * sig_gate * (1.0 - sig_gate)], 1).astype(jnp.bfloat16)
        return (carry + terms, grad_row)
    kernel_sum, grad_glu = lax.scan(fourth_pass, jnp.zeros((K, C), jnp.float32), (glu_in, lengths, d_pres))
    scale = lax.rsqrt(count)
    return (out, grad_glu, proj_sum * scale, kernel_sum * scale, sum_gain * scale, sum_bias * scale)
```

```python
import functools

import jax
import jax.numpy as jnp
from jax import lax
from jax.experimental import pallas as pl
from jax.experimental.pallas import tpu as pltpu
from jax.sharding import PartitionSpec as P

eps = 1e-05
f32 = jnp.float32
bf16 = jnp.bfloat16

NZ, NYH, NC, NYL, NX = 8, 4, 2, 2, 4
ROWS, CH, TAPS, LANES = 128, 768, 31, 128
TILES = CH // LANES
HALF = CH // 2
REACH = 16
BLOCK = CH // (NZ * NYH * NC)


def rem(a, b):
    return lax.rem(a, jnp.int32(b))


def div(a, b):
    return lax.div(a, jnp.int32(b))


def lanes_of(c, first=0):
    return pl.ds(pl.multiple_of(first + c * LANES, LANES), LANES)


def tiles(fn):
    def step(c, carry):
        fn(c)
        return carry

    lax.fori_loop(0, TILES, step, 0)


def fused(glu_hbm, len_ref, kern_hbm, gain_ref, bias_ref, w_hbm, cot_hbm,
          out_hbm, gg_hbm, gp_ref, gk_ref, gn_ref, gb_ref,
          glu, cot, kern, unit, conv, fac, dwide, da, act, out, gg,
          wblk, wfull, hs, hr, ds_, dr_, a1, a2, a3, b1, b2, b3, stat,
          kt, kr, k2, k3, kf, gown, gsend, grc, gxs, gxr, gyf, gys, gyr, gz, gzr, fin, fb,
          ssem, rsem, lsem):
    dp = lax.axis_index("dp")
    ctx = lax.axis_index("ctx")
    z, yh, core = div(dp, 8), rem(div(dp, 2), 4), rem(dp, 2)
    yl, x = div(ctx, 4), rem(ctx, 4)
    y = yh * 2 + yl
    g = x * 2 + core
    sib = 1 - core

    def dev(z_, y_, x_, c_):
        return (z_ * 8 + div(y_, 2) * 2 + c_, rem(y_, 2) * 4 + x_)

    def on_g(j):
        return dev(z, y, div(j, 2), rem(j, 2))

    def on_y(j):
        return dev(z, j, x, core)

    def on_z(j):
        return dev(j, y, x, core)

    def on_x(j):
        return dev(z, y, j, core)

    sibling = dev(z, y, x, sib)
    sends = [0]
    recvs = [0]
    pending = []

    def rsems(n):
        recvs[0] += n
        return recvs[0] - n

    def copy(src, dst, recv, target):
        sends[0] += 1
        return pltpu.make_async_remote_copy(
            src_ref=src, dst_ref=dst, send_sem=ssem.at[sends[0] - 1], recv_sem=rsem.at[recv],
            device_id=target, device_id_type=pl.DeviceIdType.MESH)

    def send(src, dst, recv, target):
        c = copy(src, dst, recv, target)
        c.start()
        pending.append(c)

    def arrived(dst, recv):
        pltpu.make_async_remote_copy(
            src_ref=dst, dst_ref=dst, send_sem=ssem.at[0], recv_sem=rsem.at[recv],
            device_id=sibling, device_id_type=pl.DeviceIdType.MESH).wait_recv()

    def exchange(buf, me, where, n=8):
        base = rsems(n)
        for d in range(1, n):
            send(buf.at[me], buf.at[me], base + d, where(rem(me + d, n)))

        def done():
            for d in range(1, n):
                arrived(buf.at[rem(me + (n - d), n)], base + d)

        return done

    loads = [pltpu.make_async_copy(a, b, lsem.at[i]) for i, (a, b) in enumerate(
        [(glu_hbm, glu), (kern_hbm, kern), (cot_hbm, cot)])]
    for c in loads:
        c.start()
    load_w = pltpu.make_async_copy(w_hbm, wblk.at[z, x, core], lsem.at[3])

    @pl.when(yh == x)
    def _():
        load_w.start()

    barrier = pltpu.get_barrier_semaphore()
    peers = [on_g(rem(g + d, 8)) for d in range(1, 8)]
    peers += [on_y(rem(y + d, 8)) for d in range(1, 8)]
    peers += [on_z(rem(z + d, 8)) for d in range(1, 8)]
    flip = yh * 2 + (1 - yl)
    peers += [dev(z, flip, div(rem(g + d, 8), 2), rem(rem(g + d, 8), 2)) for d in range(1, 8)]
    for p in peers:
        pl.semaphore_signal(barrier, inc=1, device_id=p, device_id_type=pl.DeviceIdType.MESH)

    pos0 = ctx * ROWS
    length = len_ref[0]
    n_live = jnp.clip(length - pos0, 0, ROWS).astype(f32)

    def live():
        return (lax.broadcasted_iota(jnp.int32, (ROWS, LANES), 0) + pos0 < length).astype(f32)

    loads[0].wait()

    @tiles
    def _(c):
        v = glu[:, lanes_of(c)].astype(f32)
        sg = jax.nn.sigmoid(glu[:, lanes_of(c, CH)].astype(f32))
        u = (live() * v * sg).astype(bf16)
        hs[0, :, lanes_of(c)] = u[:REACH]
        hs[1, :, lanes_of(c)] = u[ROWS - REACH:]
        unit[c, pl.ds(REACH, ROWS), :] = u.astype(f32)

    @pl.when(ctx == 0)
    def _():
        hr[0] = jnp.zeros((REACH, CH), bf16)
        dr_[0] = jnp.zeros((REACH, CH), bf16)

    @pl.when(ctx == 7)
    def _():
        hr[1] = jnp.zeros((REACH, CH), bf16)
        dr_[1] = jnp.zeros((REACH, CH), bf16)

    pl.semaphore_wait(barrier, len(peers))

    def halo(src, dst):
        base = rsems(2)
        to_left = copy(src.at[0], dst.at[1], base + 1, (dp, ctx - 1))
        to_right = copy(src.at[1], dst.at[0], base, (dp, ctx + 1))

        @pl.when(ctx > 0)
        def _():
            to_left.start()

        @pl.when(ctx < 7)
        def _():
            to_right.start()

        def done():
            @pl.when(ctx > 0)
            def _():
                arrived(dst.at[0], base)
                to_left.wait_send()

            @pl.when(ctx < 7)
            def _():
                arrived(dst.at[1], base + 1)
                to_right.wait_send()

        return done

    halo_done = halo(hs, hr)

    w1 = rsems(1)
    mine = wblk.at[z, x, core]
    w1_sends = [copy(mine, mine, w1, on_y(rem(yh + d, 4) * 2 + yl)) for d in range(1, 4)]

    @pl.when(yh == x)
    def _():
        load_w.wait()
        for c in w1_sends:
            c.start()

    @pl.when(yh != x)
    def _():
        arrived(mine, w1)

    w2 = rsems(8)
    for d in range(1, 8):
        send(mine, mine, w2 + d, on_z(rem(z + d, 8)))

    halo_done()
    loads[1].wait()

    @tiles
    def _(c):
        unit[c, pl.ds(0, REACH), :] = hr[0, :, lanes_of(c)].astype(f32)
        unit[c, pl.ds(REACH + ROWS, REACH), :] = hr[1, :, lanes_of(c)].astype(f32)
        acc = jnp.zeros((ROWS, LANES), f32)
        for k in range(TAPS):
            acc = acc + kern[pl.ds(k, 1), lanes_of(c)] * unit[c, pl.ds(k + 1, ROWS), :]
        conv[c] = acc
        m = live()
        s = jnp.sum(m * acc, 0, keepdims=True)
        centred = acc - s / jnp.maximum(n_live, 1.0)
        q = jnp.sum(m * centred * centred, 0, keepdims=True)
        n = jnp.full((1, LANES), n_live, f32)
        a1[g, :, lanes_of(c)] = jnp.concatenate([s, q, n, jnp.zeros((1, LANES), f32)], 0)

    def merged(buf):
        total = buf[0]
        for i in range(1, 8):
            total = total + buf[i]
        s, q, n = total[0:1], total[1:2], total[2:3]
        mean = s / jnp.maximum(n, 1.0)
        for i in range(8):
            off = buf[i, 0:1, :] - buf[i, 2:3, :] * mean
            q = q + off * off / jnp.maximum(buf[i, 2:3, :], 1.0)
        return s, q, n

    def summed(buf):
        total = buf[0]
        for i in range(1, 8):
            total = total + buf[i]
        return total

    a_done = exchange(a1, g, on_g)
    for d in range(1, 8):
        arrived(wblk.at[rem(z + (8 - d), 8), x, core], w2 + d)
    w3 = rsems(4)
    w4 = rsems(4)
    strip = wblk.at[:, x, core]
    for d in range(1, 4):
        send(strip, strip, w3 + d, on_x(rem(x + d, 4)))
    send(strip, strip, w4, sibling)

    zero = jnp.zeros((1, CH), f32)
    a_done()
    a2[y] = jnp.concatenate([*merged(a1), zero], 0)
    a_done = exchange(a2, y, on_y)
    a_done()
    a3[z] = jnp.concatenate([*merged(a2), zero], 0)
    a_done = exchange(a3, z, on_z)
    for d in range(1, 4):
        piece = wblk.at[:, rem(x + (4 - d), 4), core]
        arrived(piece, w3 + d)
        send(piece, piece, w4 + d, sibling)
    a_done()
    s, q, n = merged(a3)
    stat[0:1] = s / n
    stat[1:2] = lax.rsqrt(q / n + eps)
    stat[2:3] = 1.0 / n
    stat[3:4] = lax.rsqrt(n)

    @tiles
    def _(c):
        at = lanes_of(c)
        normed = (conv[c] - stat[0:1, at]) * stat[1:2, at]
        conv[c] = normed
        pre = gain_ref[0:1, at] * normed + bias_ref[0:1, at]
        sp = jax.nn.sigmoid(pre)
        m = live()
        act[:, at] = (m * pre * sp).astype(bf16)
        fac[c] = m * sp * (1.0 + pre * (1.0 - sp))

    for d in range(4):
        arrived(wblk.at[:, rem(x + (4 - d), 4), sib], w4 + d)

    def gather(i, carry):
        for p in range(2):
            rows = jnp.concatenate(
                [wblk[i, 2 * p + h, e].astype(f32) for h in range(2) for e in range(2)], 0)
            wfull[pl.ds(pl.multiple_of(i * 96 + p * 48, 16), 48), :] = rows.astype(bf16)
        return carry

    lax.fori_loop(0, NZ, gather, 0)
    loads[2].wait()
    da[...] = lax.dot_general(cot[...], wfull[...], (((1,), (1,)), ((), ())), preferred_element_type=f32)

    @tiles
    def _(c):
        at = lanes_of(c)
        d_pre = da[:, at] * fac[c]
        fac[c] = d_pre
        b1[g, :, at] = jnp.concatenate(
            [jnp.sum(d_pre, 0, keepdims=True), jnp.sum(d_pre * conv[c], 0, keepdims=True)], 0)

    b_done = exchange(b1, g, on_g)

    own_cols = pl.ds(pl.multiple_of(core * HALF, LANES), HALF)
    sib_cols = pl.ds(pl.multiple_of(sib * HALF, LANES), HALF)

    @tiles
    def _(c):
        rows = pl.ds(pl.multiple_of(c * LANES, LANES), LANES)
        a = act[:, lanes_of(c)]
        dims = (((0,), (0,)), ((), ()))
        gsend[rows, :] = lax.dot_general(a, cot[:, sib_cols], dims, preferred_element_type=f32).astype(bf16)
        gown[rows, :] = lax.dot_general(a, cot[:, own_cols], dims, preferred_element_type=f32)

    gc = rsems(1)
    send(gsend, grc, gc, sibling)

    b_done()
    b2[y] = summed(b1)
    b_done = exchange(b2, y, on_y)

    out[...] = jnp.dot(act[...], wfull[...], preferred_element_type=f32).astype(bf16)
    store_out = pltpu.make_async_copy(out, out_hbm, lsem.at[4])
    store_out.start()

    arrived(grc, gc)

    def add_core(j, carry):
        rows = pl.ds(pl.multiple_of(j * 192, 16), 192)
        t = gown[rows, :] + grc[rows, :].astype(f32)
        gown[rows, :] = t
        gxs[j] = t.astype(bf16)
        return carry

    lax.fori_loop(0, NX, add_core, 0)
    gx = rsems(4)
    for d in range(1, 4):
        j = rem(x + d, 4)
        send(gxs.at[j], gxr.at[d], gx + d, on_x(j))

    b_done()
    b3[z] = summed(b2)
    b_done = exchange(b3, z, on_z)
    b_done()
    sums = summed(b3)
    gb_ref[...] = sums[0:1] * stat[3:4]
    gn_ref[...] = sums[1:2] * stat[3:4]
    stat[4:5] = sums[0:1] * stat[2:3]
    stat[5:6] = sums[1:2] * stat[2:3]

    @tiles
    def _(c):
        at = lanes_of(c)
        d = (live() * (gain_ref[0:1, at] * stat[1:2, at])
             * (fac[c] - stat[4:5, at] - conv[c] * stat[5:6, at])).astype(bf16)
        ds_[0, :, at] = d[:REACH]
        ds_[1, :, at] = d[ROWS - REACH:]
        dwide[c, pl.ds(REACH, ROWS), :] = d.astype(f32)

    halo_done = halo(ds_, dr_)

    @tiles
    def _(c):
        at = lanes_of(c)
        d = dwide[c, pl.ds(REACH, ROWS), :]
        for k in range(TAPS):
            kt[k // 4, pl.ds(k % 4, 1), at] = jnp.sum(d * unit[c, pl.ds(k + 1, ROWS), :], 0, keepdims=True)
        kt[7, 3:4, at] = jnp.zeros((1, LANES), f32)

    k1 = rsems(8)
    for d in range(1, 8):
        j = rem(g + d, 8)
        send(kt.at[j], kr.at[d], k1 + d, on_g(j))

    for d in range(1, 4):
        arrived(gxr.at[d], gx + d)
    t = gown[pl.ds(pl.multiple_of(x * 192, 16), 192), :]
    for d in range(1, 4):
        t = t + gxr[d].astype(f32)
    t = t.reshape(24, 8, HALF)
    gyf[...] = t
    gys[...] = t.astype(bf16)
    gy = rsems(8)
    for d in range(1, 8):
        j = rem(y + d, 8)
        send(gys.at[pl.ds(rem(j, 2) * 12 + div(j, 2) * 3, 3)], gyr.at[d], gy + d, on_y(j))

    halo_done()

    @tiles
    def _(c):
        at = lanes_of(c)
        dwide[c, pl.ds(0, REACH), :] = dr_[0, :, at].astype(f32)
        dwide[c, pl.ds(REACH + ROWS, REACH), :] = dr_[1, :, at].astype(f32)
        acc = jnp.zeros((ROWS, LANES), f32)
        for k in range(TAPS):
            acc = acc + kern[pl.ds(k, 1), at] * dwide[c, pl.ds(TAPS - k, ROWS), :]
        v = glu[:, at].astype(f32)
        sg = jax.nn.sigmoid(glu[:, lanes_of(c, CH)].astype(f32))
        du = live() * acc * sg
        gg[:, at] = du.astype(bf16)
        gg[:, lanes_of(c, CH)] = (du * v * (1.0 - sg)).astype(bf16)

    store_gg = pltpu.make_async_copy(gg, gg_hbm, lsem.at[5])
    store_gg.start()

    for d in range(1, 8):
        arrived(kr.at[d], k1 + d)
    t = kt[g]
    for d in range(1, 8):
        t = t + kr[d]
    k2[y] = t
    k_done = exchange(k2, y, on_y)

    for d in range(1, 8):
        arrived(gyr.at[d], gy + d)
    t = gyf[pl.ds(yl * 12 + yh * 3, 3)]
    for d in range(1, 8):
        t = t + gyr[d].astype(f32)
    gz[...] = t
    owner = 2 * x + yl
    gzb = rsems(8)
    slot = rem(z + 8 - owner, 8)
    to_owner = copy(gz, gzr.at[slot], gzb + slot, on_z(owner))

    @pl.when(z != owner)
    def _():
        to_owner.start()

    k_done()
    k3[z] = summed(k2)
    k_done = exchange(k3, z, on_z)

    fbb = rsems(2)
    spread = []
    for d in range(1, 16):
        e = rem(core + d, 2)
        c_ = rem(ctx + d // 2, 8)
        spread.append(copy(fin.at[pl.ds(e, 2)], fb.at[core], fbb + core, (div(dp, 2) * 2 + e, c_)))

    @pl.when(z == owner)
    def _():
        t = gz[...]
        for d in range(1, 8):
            arrived(gzr.at[d], gzb + d)
            t = t + gzr[d]
        fin[...] = t * stat[3:4, 0:HALF].reshape(1, 1, HALF)
        for c in spread:
            c.start()
        fb[core] = fin[pl.ds(core, 2)]

    k_done()
    kf[g] = summed(k3) * stat[3:4]
    k_done = exchange(kf, g, on_g)
    k_done()
    for j in range(8):
        w = 4 if j < 7 else 3
        gk_ref[pl.ds(4 * j, w), :] = kf[j, 0:w, :]

    @pl.when(z != owner)
    def _():
        arrived(fb.at[core], fbb + core)

    arrived(fb.at[sib], fbb + sib)
    for h in range(2):
        v = fb[h].reshape(16, HALF)
        gp_ref[:, pl.ds(h * HALF, HALF)] = jnp.where(core == 0, v[0:BLOCK], v[16 - BLOCK:16])

    for c in pending:
        c.wait_send()

    @pl.when(yh == x)
    def _():
        for c in w1_sends:
            c.wait_send()

    @pl.when(z != owner)
    def _():
        to_owner.wait_send()

    @pl.when(z == owner)
    def _():
        for c in spread:
            c.wait_send()

    store_out.wait()
    store_gg.wait()


def body(glu_in, lengths, kernel, bn_gain, bn_bias, proj_weight, cotangent):
    vm = pltpu.VMEM
    anyspec = pl.BlockSpec(memory_space=pl.ANY)
    vspec = pl.BlockSpec(memory_space=pltpu.VMEM)
    sspec = pl.BlockSpec(memory_space=pltpu.SMEM)
    scratch = [
        vm((ROWS, 2 * CH), bf16), vm((ROWS, CH), bf16), vm((TAPS, CH), f32),
        vm((TILES, ROWS + 2 * REACH, LANES), f32), vm((TILES, ROWS, LANES), f32),
        vm((TILES, ROWS, LANES), f32), vm((TILES, ROWS + 2 * REACH, LANES), f32),
        vm((ROWS, CH), f32), vm((ROWS, CH), bf16), vm((ROWS, CH), bf16), vm((ROWS, 2 * CH), bf16),
        vm((NZ, NYH, NC, BLOCK, CH), bf16), vm((CH, CH), bf16),
        vm((2, REACH, CH), bf16), vm((2, REACH, CH), bf16), vm((2, REACH, CH), bf16), vm((2, REACH, CH), bf16),
        vm((8, 4, CH), f32), vm((8, 4, CH), f32), vm((8, 4, CH), f32),
        vm((8, 2, CH), f32), vm((8, 2, CH), f32), vm((8, 2, CH), f32),
        vm((8, CH), f32),
        vm((8, 4, CH), f32), vm((8, 4, CH), f32), vm((8, 4, CH), f32), vm((8, 4, CH), f32), vm((8, 4, CH), f32),
        vm((CH, HALF), f32), vm((CH, HALF), bf16), vm((CH, HALF), bf16),
        vm((NX, 192, HALF), bf16), vm((NX, 192, HALF), bf16),
        vm((24, 8, HALF), f32), vm((24, 8, HALF), bf16), vm((8, 3, 8, HALF), bf16),
        vm((3, 8, HALF), f32), vm((8, 3, 8, HALF), f32), vm((3, 8, HALF), f32), vm((2, 2, 8, HALF), f32),
        pltpu.SemaphoreType.DMA((160,)), pltpu.SemaphoreType.DMA((160,)), pltpu.SemaphoreType.DMA((6,)),
    ]
    outs = [
        jax.ShapeDtypeStruct((ROWS, CH), bf16),
        jax.ShapeDtypeStruct((ROWS, 2 * CH), bf16),
        jax.ShapeDtypeStruct((BLOCK, CH), f32),
        jax.ShapeDtypeStruct((TAPS, CH), f32),
        jax.ShapeDtypeStruct((1, CH), f32),
        jax.ShapeDtypeStruct((1, CH), f32),
    ]
    result, grad_glu, grad_proj, grad_kernel, grad_gain, grad_bias = pl.pallas_call(
        fused,
        out_shape=outs,
        in_specs=[anyspec, sspec, anyspec, vspec, vspec, anyspec, anyspec],
        out_specs=[anyspec, anyspec, vspec, vspec, vspec, vspec],
        scratch_shapes=scratch,
        compiler_params=pltpu.CompilerParams(
            collective_id=0, has_side_effects=True, vmem_limit_bytes=48 * 1024 * 1024),
        name="conformer_conv",
    )(glu_in[0], lengths, kernel, bn_gain[None], bn_bias[None], proj_weight, cotangent[0])
    return (result[None], grad_glu[None], grad_proj, grad_kernel, grad_gain[0], grad_bias[0])


def solution(mesh):
    in_specs = (P("dp", "ctx", None), P("dp"), P(), P(), P(), P("dp", None), P("dp", "ctx", None))
    out_specs = (P("dp", "ctx", None), P("dp", "ctx", None), P("dp", None), P(), P(), P())
    return jax.shard_map(body, mesh=mesh, in_specs=in_specs, out_specs=out_specs, check_vma=False)
```

```python
import functools

import jax
import jax.numpy as jnp
from jax import lax
from jax.experimental import pallas as pl
from jax.experimental.pallas import tpu as pltpu
from jax.sharding import PartitionSpec as P

eps = 1e-05
f32 = jnp.float32
bf16 = jnp.bfloat16

NZ, NYH, NC, NYL, NX = 8, 4, 2, 2, 4
ROWS, CH, TAPS, LANES = 128, 768, 31, 128
TILES = CH // LANES
HALF = CH // 2
REACH = 16
BLOCK = CH // (NZ * NYH * NC)


def rem(a, b):
    return lax.rem(a, jnp.int32(b))


def div(a, b):
    return lax.div(a, jnp.int32(b))


def lanes_of(c, first=0):
    return pl.ds(pl.multiple_of(first + c * LANES, LANES), LANES)


def tiles(fn):
    def step(c, carry):
        fn(c)
        return carry

    lax.fori_loop(0, TILES, step, 0)


def fused(glu_hbm, len_ref, kern_hbm, gain_in, bias_in, w_hbm, cot_hbm,
          out_hbm, gg_hbm, gp_ref, gk_ref, gn_ref, gb_ref,
          glu, cot, kern, unit, conv, fac, dwide, da, act, out, gg,
          wblk, wfull, hs, hr, ds_, dr_, a1, a2, a3, b1, b2, b3, stat,
          kt, kr, k2, k3, kf, gown, gsend, grc, gxs, gxr, gyf, gys, gyr, gz, gzr, fin, fb,
          gain_v, bias_v, ssem, rsem, lsem):
    dp = lax.axis_index("dp")
    ctx = lax.axis_index("ctx")
    z, yh, core = div(dp, 8), rem(div(dp, 2), 4), rem(dp, 2)
    yl, x = div(ctx, 4), rem(ctx, 4)
    y = yh * 2 + yl
    g = x * 2 + core
    sib = 1 - core

    def dev(z_, y_, x_, c_):
        return (z_ * 8 + div(y_, 2) * 2 + c_, rem(y_, 2) * 4 + x_)

    def on_g(j):
        return dev(z, y, div(j, 2), rem(j, 2))

    def on_y(j):
        return dev(z, j, x, core)

    def on_z(j):
        return dev(j, y, x, core)

    def on_x(j):
        return dev(z, y, j, core)

    sibling = dev(z, y, x, sib)
    sends = [0]
    recvs = [0]
    pending = []
    cond = []

    def rsems(n):
        recvs[0] += n
        return recvs[0] - n

    def copy(src, dst, recv, target):
        sends[0] += 1
        return pltpu.make_async_remote_copy(
            src_ref=src, dst_ref=dst, send_sem=ssem.at[sends[0] - 1], recv_sem=rsem.at[recv],
            device_id=target, device_id_type=pl.DeviceIdType.MESH)

    def send(src, dst, recv, target):
        c = copy(src, dst, recv, target)
        c.start()
        pending.append(c)

    def arrived(dst, recv):
        pltpu.make_async_remote_copy(
            src_ref=dst, dst_ref=dst, send_sem=ssem.at[0], recv_sem=rsem.at[recv],
            device_id=sibling, device_id_type=pl.DeviceIdType.MESH).wait_recv()

    def finish():
        for c in pending:
            c.wait_send()
        for when, copies in cond:
            @pl.when(when)
            def _():
                for c in copies:
                    c.wait_send()

    def exchange(buf, me, where, n=8):
        base = rsems(n)
        for d in range(1, n):
            send(buf.at[me], buf.at[me], base + d, where(rem(me + d, n)))

        def done():
            for d in range(1, n):
                arrived(buf.at[rem(me + (n - d), n)], base + d)

        return done

    loads = [pltpu.make_async_copy(a, b, lsem.at[i]) for i, (a, b) in enumerate(
        [(glu_hbm, glu), (kern_hbm, kern), (cot_hbm, cot), (gain_in, gain_v), (bias_in, bias_v)])]
    for c in loads:
        c.start()
    load_w = pltpu.make_async_copy(w_hbm, wblk.at[z, x, core], lsem.at[5])

    @pl.when(yh == x)
    def _():
        load_w.start()

    barrier = pltpu.get_barrier_semaphore()
    peers = [on_g(rem(g + d, 8)) for d in range(1, 8)]
    peers += [on_y(rem(y + d, 8)) for d in range(1, 8)]
    peers += [on_z(rem(z + d, 8)) for d in range(1, 8)]
    flip = yh * 2 + (1 - yl)
    peers += [dev(z, flip, div(rem(g + d, 8), 2), rem(rem(g + d, 8), 2)) for d in range(1, 8)]
    for p in peers:
        pl.semaphore_signal(barrier, inc=1, device_id=p, device_id_type=pl.DeviceIdType.MESH)

    pos0 = ctx * ROWS
    length = len_ref[0]
    n_live = jnp.clip(length - pos0, 0, ROWS).astype(f32)

    def live():
        return (lax.broadcasted_iota(jnp.int32, (ROWS, LANES), 0) + pos0 < length).astype(f32)

    loads[0].wait()

    @tiles
    def _(c):
        v = glu[:, lanes_of(c)].astype(f32)
        sg = jax.nn.sigmoid(glu[:, lanes_of(c, CH)].astype(f32))
        u = (live() * v * sg).astype(bf16)
        hs[0, :, lanes_of(c)] = u[:REACH]
        hs[1, :, lanes_of(c)] = u[ROWS - REACH:]
        unit[c, pl.ds(REACH, ROWS), :] = u.astype(f32)

    @pl.when(ctx == 0)
    def _():
        hr[0] = jnp.zeros((REACH, CH), bf16)
        dr_[0] = jnp.zeros((REACH, CH), bf16)

    @pl.when(ctx == 7)
    def _():
        hr[1] = jnp.zeros((REACH, CH), bf16)
        dr_[1] = jnp.zeros((REACH, CH), bf16)

    pl.semaphore_wait(barrier, len(peers))

    def halo(src, dst):
        base = rsems(2)
        to_left = copy(src.at[0], dst.at[1], base + 1, (dp, ctx - 1))
        to_right = copy(src.at[1], dst.at[0], base, (dp, ctx + 1))

        @pl.when(ctx > 0)
        def _():
            to_left.start()

        @pl.when(ctx < 7)
        def _():
            to_right.start()

        def done():
            @pl.when(ctx > 0)
            def _():
                arrived(dst.at[0], base)
                to_left.wait_send()

            @pl.when(ctx < 7)
            def _():
                arrived(dst.at[1], base + 1)
                to_right.wait_send()

        return done

    halo_done = halo(hs, hr)

    w1 = rsems(1)
    mine = wblk.at[z, x, core]
    w1_sends = [copy(mine, mine, w1, on_y(rem(yh + d, 4) * 2 + yl)) for d in range(1, 4)]

    cond.append((yh == x, w1_sends))

    @pl.when(yh == x)
    def _():
        load_w.wait()
        for c in w1_sends:
            c.start()

    @pl.when(yh != x)
    def _():
        arrived(mine, w1)

    w2 = rsems(8)
    for d in range(1, 8):
        send(mine, mine, w2 + d, on_z(rem(z + d, 8)))

    halo_done()
    for c in (loads[1], loads[3], loads[4]):
        c.wait()
    stat[6:7] = gain_v[...].reshape(1, CH)
    stat[7:8] = bias_v[...].reshape(1, CH)

    @tiles
    def _(c):
        unit[c, pl.ds(0, REACH), :] = hr[0, :, lanes_of(c)].astype(f32)
        unit[c, pl.ds(REACH + ROWS, REACH), :] = hr[1, :, lanes_of(c)].astype(f32)
        acc = jnp.zeros((ROWS, LANES), f32)
        for k in range(TAPS):
            acc = acc + kern[pl.ds(k, 1), lanes_of(c)] * unit[c, pl.ds(k + 1, ROWS), :]
        conv[c] = acc
        m = live()
        s = jnp.sum(m * acc, 0, keepdims=True)
        centred = acc - s / jnp.maximum(n_live, 1.0)
        q = jnp.sum(m * centred * centred, 0, keepdims=True)
        n = jnp.full((1, LANES), n_live, f32)
        a1[g, :, lanes_of(c)] = jnp.concatenate([s, q, n, jnp.zeros((1, LANES), f32)], 0)

    def merged(buf):
        total = buf[0]
        for i in range(1, 8):
            total = total + buf[i]
        s, q, n = total[0:1], total[1:2], total[2:3]
        mean = s / jnp.maximum(n, 1.0)
        for i in range(8):
            off = buf[i, 0:1, :] - buf[i, 2:3, :] * mean
            q = q + off * off / jnp.maximum(buf[i, 2:3, :], 1.0)
        return s, q, n

    def summed(buf):
        total = buf[0]
        for i in range(1, 8):
            total = total + buf[i]
        return total

    a_done = exchange(a1, g, on_g)
    for d in range(1, 8):
        arrived(wblk.at[rem(z + (8 - d), 8), x, core], w2 + d)
    w3 = rsems(4)
    w4 = rsems(4)
    strip = wblk.at[:, x, core]
    for d in range(1, 4):
        send(strip, strip, w3 + d, on_x(rem(x + d, 4)))
    send(strip, strip, w4, sibling)

    zero = jnp.zeros((1, CH), f32)
    a_done()
    a2[y] = jnp.concatenate([*merged(a1), zero], 0)
    a_done = exchange(a2, y, on_y)
    a_done()
    a3[z] = jnp.concatenate([*merged(a2), zero], 0)
    a_done = exchange(a3, z, on_z)
    for d in range(1, 4):
        piece = wblk.at[:, rem(x + (4 - d), 4), core]
        arrived(piece, w3 + d)
        send(piece, piece, w4 + d, sibling)
    a_done()
    s, q, n = merged(a3)
    stat[0:1] = s / n
    stat[1:2] = lax.rsqrt(q / n + eps)
    stat[2:3] = 1.0 / n
    stat[3:4] = lax.rsqrt(n)

    @tiles
    def _(c):
        at = lanes_of(c)
        normed = (conv[c] - stat[0:1, at]) * stat[1:2, at]
        conv[c] = normed
        pre = stat[6:7, at] * normed + stat[7:8, at]
        sp = jax.nn.sigmoid(pre)
        m = live()
        act[:, at] = (m * pre * sp).astype(bf16)
        fac[c] = m * sp * (1.0 + pre * (1.0 - sp))

    for d in range(4):
        arrived(wblk.at[:, rem(x + (4 - d), 4), sib], w4 + d)

    def gather(i, carry):
        for p in range(2):
            rows = jnp.concatenate(
                [wblk[i, 2 * p + h, e].astype(f32) for h in range(2) for e in range(2)], 0)
            wfull[pl.ds(pl.multiple_of(i * 96 + p * 48, 16), 48), :] = rows.astype(bf16)
        return carry

    lax.fori_loop(0, NZ, gather, 0)
    loads[2].wait()
    da[...] = lax.dot_general(cot[...], wfull[...], (((1,), (1,)), ((), ())), preferred_element_type=f32)

    @tiles
    def _(c):
        at = lanes_of(c)
        d_pre = da[:, at] * fac[c]
        fac[c] = d_pre
        b1[g, :, at] = jnp.concatenate(
            [jnp.sum(d_pre, 0, keepdims=True), jnp.sum(d_pre * conv[c], 0, keepdims=True)], 0)

    b_done = exchange(b1, g, on_g)

    own_cols = pl.ds(pl.multiple_of(core * HALF, LANES), HALF)
    sib_cols = pl.ds(pl.multiple_of(sib * HALF, LANES), HALF)

    @tiles
    def _(c):
        rows = pl.ds(pl.multiple_of(c * LANES, LANES), LANES)
        a = act[:, lanes_of(c)]
        dims = (((0,), (0,)), ((), ()))
        gsend[rows, :] = lax.dot_general(a, cot[:, sib_cols], dims, preferred_element_type=f32).astype(bf16)
        gown[rows, :] = lax.dot_general(a, cot[:, own_cols], dims, preferred_element_type=f32)

    gc = rsems(1)
    send(gsend, grc, gc, sibling)

    b_done()
    b2[y] = summed(b1)
    b_done = exchange(b2, y, on_y)

    out[...] = jnp.dot(act[...], wfull[...], preferred_element_type=f32).astype(bf16)
    store_out = pltpu.make_async_copy(out, out_hbm, lsem.at[6])
    store_out.start()

    arrived(grc, gc)

    def add_core(j, carry):
        rows = pl.ds(pl.multiple_of(j * 192, 16), 192)
        t = gown[rows, :] + grc[rows, :].astype(f32)
        gown[rows, :] = t
        gxs[j] = t.astype(bf16)
        return carry

    lax.fori_loop(0, NX, add_core, 0)
    gx = rsems(4)
    for d in range(1, 4):
        j = rem(x + d, 4)
        send(gxs.at[j], gxr.at[d], gx + d, on_x(j))

    b_done()
    b3[z] = summed(b2)
    b_done = exchange(b3, z, on_z)
    b_done()
    sums = summed(b3)
    gb_ref[...] = (sums[0:1] * stat[3:4]).reshape(CH)
    gn_ref[...] = (sums[1:2] * stat[3:4]).reshape(CH)
    stat[4:5] = sums[0:1] * stat[2:3]
    stat[5:6] = sums[1:2] * stat[2:3]

    @tiles
    def _(c):
        at = lanes_of(c)
        d = (live() * (stat[6:7, at] * stat[1:2, at])
             * (fac[c] - stat[4:5, at] - conv[c] * stat[5:6, at])).astype(bf16)
        ds_[0, :, at] = d[:REACH]
        ds_[1, :, at] = d[ROWS - REACH:]
        dwide[c, pl.ds(REACH, ROWS), :] = d.astype(f32)

    halo_done = halo(ds_, dr_)

    @tiles
    def _(c):
        at = lanes_of(c)
        d = dwide[c, pl.ds(REACH, ROWS), :]
        for k in range(TAPS):
            kt[k // 4, pl.ds(k % 4, 1), at] = jnp.sum(d * unit[c, pl.ds(k + 1, ROWS), :], 0, keepdims=True)
        kt[7, 3:4, at] = jnp.zeros((1, LANES), f32)

    k1 = rsems(8)
    for d in range(1, 8):
        j = rem(g + d, 8)
        send(kt.at[j], kr.at[d], k1 + d, on_g(j))

    for d in range(1, 4):
        arrived(gxr.at[d], gx + d)
    t = gown[pl.ds(pl.multiple_of(x * 192, 16), 192), :]
    for d in range(1, 4):
        t = t + gxr[d].astype(f32)
    t = t.reshape(24, 8, HALF)
    gyf[...] = t
    gys[...] = t.astype(bf16)
    gy = rsems(8)
    for d in range(1, 8):
        j = rem(y + d, 8)
        send(gys.at[pl.ds(rem(j, 2) * 12 + div(j, 2) * 3, 3)], gyr.at[d], gy + d, on_y(j))

    halo_done()

    @tiles
    def _(c):
        at = lanes_of(c)
        dwide[c, pl.ds(0, REACH), :] = dr_[0, :, at].astype(f32)
        dwide[c, pl.ds(REACH + ROWS, REACH), :] = dr_[1, :, at].astype(f32)
        acc = jnp.zeros((ROWS, LANES), f32)
        for k in range(TAPS):
            acc = acc + kern[pl.ds(k, 1), at] * dwide[c, pl.ds(TAPS - k, ROWS), :]
        v = glu[:, at].astype(f32)
        sg = jax.nn.sigmoid(glu[:, lanes_of(c, CH)].astype(f32))
        du = live() * acc * sg
        gg[:, at] = du.astype(bf16)
        gg[:, lanes_of(c, CH)] = (du * v * (1.0 - sg)).astype(bf16)

    store_gg = pltpu.make_async_copy(gg, gg_hbm, lsem.at[7])
    store_gg.start()

    for d in range(1, 8):
        arrived(kr.at[d], k1 + d)
    t = kt[g]
    for d in range(1, 8):
        t = t + kr[d]
    k2[y] = t
    k_done = exchange(k2, y, on_y)

    for d in range(1, 8):
        arrived(gyr.at[d], gy + d)
    t = gyf[pl.ds(yl * 12 + yh * 3, 3)]
    for d in range(1, 8):
        t = t + gyr[d].astype(f32)
    gz[...] = t
    owner = 2 * x + yl
    gzb = rsems(8)
    slot = rem(z + 8 - owner, 8)
    to_owner = copy(gz, gzr.at[slot], gzb + slot, on_z(owner))

    cond.append((z != owner, [to_owner]))

    @pl.when(z != owner)
    def _():
        to_owner.start()

    k_done()
    k3[z] = summed(k2)
    k_done = exchange(k3, z, on_z)

    fbb = rsems(2)
    spread = []
    for d in range(1, 16):
        e = rem(core + d, 2)
        c_ = rem(ctx + d // 2, 8)
        spread.append(copy(fin.at[pl.ds(e, 2)], fb.at[core], fbb + core, (div(dp, 2) * 2 + e, c_)))

    cond.append((z == owner, spread))

    @pl.when(z == owner)
    def _():
        t = gz[...]
        for d in range(1, 8):
            arrived(gzr.at[d], gzb + d)
            t = t + gzr[d]
        fin[...] = t * stat[3:4, 0:HALF].reshape(1, 1, HALF)
        for c in spread:
            c.start()
        fb[core] = fin[pl.ds(core, 2)]

    k_done()
    kf[g] = summed(k3) * stat[3:4]
    k_done = exchange(kf, g, on_g)
    k_done()
    for j in range(8):
        w = 4 if j < 7 else 3
        gk_ref[pl.ds(4 * j, w), :] = kf[j, 0:w, :]

    @pl.when(z != owner)
    def _():
        arrived(fb.at[core], fbb + core)

    arrived(fb.at[sib], fbb + sib)
    for h in range(2):
        v = fb[h].reshape(16, HALF)
        gp_ref[:, pl.ds(h * HALF, HALF)] = jnp.where(core == 0, v[0:BLOCK], v[16 - BLOCK:16])

    finish()
    store_out.wait()
    store_gg.wait()


def handed_on(*refs):
    sem = refs[12]
    copies = [pltpu.make_async_copy(refs[i], refs[6 + i], sem.at[i]) for i in range(6)]
    for c in copies:
        c.start()
    for c in copies:
        c.wait()


def body(glu_in, lengths, kernel, bn_gain, bn_bias, proj_weight, cotangent):
    vm = pltpu.VMEM
    hbm = functools.partial(pltpu.with_memory_space_constraint, memory_space=pltpu.HBM)
    anyspec = pl.BlockSpec(memory_space=pl.ANY)
    vspec = pl.BlockSpec(memory_space=pltpu.VMEM)
    sspec = pl.BlockSpec(memory_space=pltpu.SMEM)
    scratch = [
        vm((ROWS, 2 * CH), bf16), vm((ROWS, CH), bf16), vm((TAPS, CH), f32),
        vm((TILES, ROWS + 2 * REACH, LANES), f32), vm((TILES, ROWS, LANES), f32),
        vm((TILES, ROWS, LANES), f32), vm((TILES, ROWS + 2 * REACH, LANES), f32),
        vm((ROWS, CH), f32), vm((ROWS, CH), bf16), vm((ROWS, CH), bf16), vm((ROWS, 2 * CH), bf16),
        vm((NZ, NYH, NC, BLOCK, CH), bf16), vm((CH, CH), bf16),
        vm((2, REACH, CH), bf16), vm((2, REACH, CH), bf16), vm((2, REACH, CH), bf16), vm((2, REACH, CH), bf16),
        vm((8, 4, CH), f32), vm((8, 4, CH), f32), vm((8, 4, CH), f32),
        vm((8, 2, CH), f32), vm((8, 2, CH), f32), vm((8, 2, CH), f32),
        vm((8, CH), f32),
        vm((8, 4, CH), f32), vm((8, 4, CH), f32), vm((8, 4, CH), f32), vm((8, 4, CH), f32), vm((8, 4, CH), f32),
        vm((CH, HALF), f32), vm((CH, HALF), bf16), vm((CH, HALF), bf16),
        vm((NX, 192, HALF), bf16), vm((NX, 192, HALF), bf16),
        vm((24, 8, HALF), f32), vm((24, 8, HALF), bf16), vm((8, 3, 8, HALF), bf16),
        vm((3, 8, HALF), f32), vm((8, 3, 8, HALF), f32), vm((3, 8, HALF), f32), vm((2, 2, 8, HALF), f32),
        vm((CH,), f32), vm((CH,), f32),
        pltpu.SemaphoreType.DMA((160,)), pltpu.SemaphoreType.DMA((160,)), pltpu.SemaphoreType.DMA((8,)),
    ]
    outs = [
        jax.ShapeDtypeStruct((ROWS, CH), bf16),
        jax.ShapeDtypeStruct((ROWS, 2 * CH), bf16),
        jax.ShapeDtypeStruct((BLOCK, CH), f32),
        jax.ShapeDtypeStruct((TAPS, CH), f32),
        jax.ShapeDtypeStruct((CH,), f32),
        jax.ShapeDtypeStruct((CH,), f32),
    ]
    results = pl.pallas_call(
        fused,
        out_shape=outs,
        in_specs=[anyspec, sspec, anyspec, anyspec, anyspec, anyspec, anyspec],
        out_specs=[anyspec, anyspec, vspec, vspec, vspec, vspec],
        scratch_shapes=scratch,
        compiler_params=pltpu.CompilerParams(
            collective_id=0, has_side_effects=True, vmem_limit_bytes=40 * 1024 * 1024),
        name="conformer_conv",
    )(hbm(glu_in[0]), lengths, hbm(kernel), hbm(bn_gain), hbm(bn_bias), hbm(proj_weight), hbm(cotangent[0]))
    result, grad_glu, grad_proj, grad_kernel, grad_gain, grad_bias = pl.pallas_call(
        handed_on,
        out_shape=outs,
        in_specs=[anyspec] * 6,
        out_specs=[anyspec] * 6,
        scratch_shapes=[pltpu.SemaphoreType.DMA((6,))],
        compiler_params=pltpu.CompilerParams(vmem_limit_bytes=1024 * 1024),
        name="handed_on",
    )(*results)
    return (result[None], grad_glu[None], grad_proj, grad_kernel, grad_gain, grad_bias)


def solution(mesh):
    in_specs = (P("dp", "ctx", None), P("dp"), P(), P(), P(), P("dp", None), P("dp", "ctx", None))
    out_specs = (P("dp", "ctx", None), P("dp", "ctx", None), P("dp", None), P(), P(), P())
    return jax.shard_map(body, mesh=mesh, in_specs=in_specs, out_specs=out_specs, check_vma=False)
```

```python
import functools

import jax
import jax.numpy as jnp
from jax import lax
from jax.experimental import pallas as pl
from jax.experimental.pallas import tpu as pltpu
from jax.sharding import PartitionSpec as P

eps = 1e-05
f32 = jnp.float32
bf16 = jnp.bfloat16

NZ, NYH, NC, NYL, NX = 8, 4, 2, 2, 4
ROWS, CH, TAPS, LANES = 128, 768, 31, 128
TILES = CH // LANES
HALF = CH // 2
REACH = 16
BLOCK = CH // (NZ * NYH * NC)
CHUNKS = HALF // LANES
NEAR = (0, 1, 7, 2, 6, 3, 5, 4)


def rem(a, b):
    return lax.rem(a, jnp.int32(b))


def div(a, b):
    return lax.div(a, jnp.int32(b))


def lanes_of(c, first=0):
    return pl.ds(pl.multiple_of(first + c * LANES, LANES), LANES)


def tiles(fn):
    def step(c, carry):
        fn(c)
        return carry

    lax.fori_loop(0, TILES, step, 0)


def fused(glu_hbm, len_ref, kern_hbm, gain_in, bias_in, w_hbm, cot_hbm,
          out_hbm, gg_hbm, gp_ref, gk_ref, gn_ref, gb_ref,
          glu, cot, kern, unit, conv, fac, dwide, da, act, out, gg, ub,
          wl, wr, wb, wfull, hs, hr, ds_, dr_, a1, a2, a3, b1, b2, b3, stat,
          kt, kr, k2, k3, kf, uq, ur, u2, gown, gsend, grc, gxs, gxr, gyf, gys, gyr, gz, gzr, fin, fb,
          gain_v, bias_v, ssem, rsem, lsem):
    dp = lax.axis_index("dp")
    ctx = lax.axis_index("ctx")
    z, yh, core = div(dp, 8), rem(div(dp, 2), 4), rem(dp, 2)
    yl, x = div(ctx, 4), rem(ctx, 4)
    y = yh * 2 + yl
    g = x * 2 + core
    sib = 1 - core

    def dev(z_, y_, x_, c_):
        return (z_ * 8 + div(y_, 2) * 2 + c_, rem(y_, 2) * 4 + x_)

    def on_g(j):
        return dev(z, y, div(j, 2), rem(j, 2))

    def on_y(j):
        return dev(z, j, x, core)

    def on_z(j):
        return dev(j, y, x, core)

    def on_x(j):
        return dev(z, y, j, core)

    sibling = dev(z, y, x, sib)
    sends = [0]
    recvs = [0]
    pending = []
    cond = []

    def rsems(n):
        recvs[0] += n
        return recvs[0] - n

    def copy(src, dst, recv, target):
        sends[0] += 1
        return pltpu.make_async_remote_copy(
            src_ref=src, dst_ref=dst, send_sem=ssem.at[sends[0] - 1], recv_sem=rsem.at[recv],
            device_id=target, device_id_type=pl.DeviceIdType.MESH)

    def send(src, dst, recv, target):
        c = copy(src, dst, recv, target)
        c.start()
        pending.append(c)

    def arrived(dst, recv):
        pltpu.make_async_remote_copy(
            src_ref=dst, dst_ref=dst, send_sem=ssem.at[0], recv_sem=rsem.at[recv],
            device_id=sibling, device_id_type=pl.DeviceIdType.MESH).wait_recv()

    def finish():
        for c in pending:
            c.wait_send()
        for when, copies in cond:
            @pl.when(when)
            def _():
                for c in copies:
                    c.wait_send()

    def exchange(buf, me, where, n=8):
        base = rsems(n)
        for d in range(1, n):
            send(buf.at[me], buf.at[me], base + d, where(rem(me + d, n)))

        def done():
            for d in range(1, n):
                arrived(buf.at[rem(me + (n - d), n)], base + d)

        return done

    barrier = pltpu.get_barrier_semaphore()
    peers = [on_g(rem(g + d, 8)) for d in range(1, 8)]
    peers += [on_y(rem(y + d, 8)) for d in range(1, 8)]
    peers += [on_z(rem(z + d, 8)) for d in range(1, 8)]
    flip = yh * 2 + (1 - yl)
    peers += [dev(z, rem(y + 2 * d, 8), x, sib) for d in range(1, 4)]
    peers += [dev(z, flip, div(rem(g + d, 8), 2), rem(rem(g + d, 8), 2)) for d in range(1, 8)]
    for p in peers:
        pl.semaphore_signal(barrier, inc=1, device_id=p, device_id_type=pl.DeviceIdType.MESH)

    loads = [pltpu.make_async_copy(a, b, lsem.at[i]) for i, (a, b) in enumerate(
        [(glu_hbm, glu), (kern_hbm, kern), (cot_hbm, cot), (gain_in, gain_v), (bias_in, bias_v)])]
    load_w = pltpu.make_async_copy(w_hbm, wl, lsem.at[5])

    @pl.when(yh == x)
    def _():
        load_w.start()

    for c in loads:
        c.start()

    pos0 = ctx * ROWS
    length = len_ref[0]
    n_live = jnp.clip(length - pos0, 0, ROWS).astype(f32)

    def live():
        return (lax.broadcasted_iota(jnp.int32, (ROWS, LANES), 0) + pos0 < length).astype(f32)

    pl.semaphore_wait(barrier, len(peers))

    own_cols = pl.ds(pl.multiple_of(core * HALF, LANES), HALF)
    sib_cols = pl.ds(pl.multiple_of(sib * HALF, LANES), HALF)
    w1, w2, w3, w4 = rsems(2), rsems(8), rsems(8), rsems(8)
    mine = wb.at[core, x, 0]
    w1_sends = [copy(wl.at[:, sib_cols], wr.at[core], w1 + core, sibling)]
    for d in range(1, 4):
        y_ = rem(yh + d, 4) * 2 + yl
        w1_sends.append(copy(wl.at[:, own_cols], wr.at[core], w1 + core, dev(z, y_, x, core)))
        w1_sends.append(copy(wl.at[:, sib_cols], wr.at[core], w1 + core, dev(z, y_, x, sib)))
    cond.append((yh == x, w1_sends))

    @pl.when(yh == x)
    def _():
        load_w.wait()
        for c in w1_sends:
            c.start()
        wr[core] = wl[:, own_cols]

    def w1_done():
        @pl.when(yh != x)
        def _():
            arrived(wr.at[core], w1 + core)

        arrived(wr.at[sib], w1 + sib)
        rows = jnp.concatenate([wr[0].astype(f32), wr[1].astype(f32)], 0)
        wb[core, x, 0] = rows.reshape(3, 8, HALF).astype(bf16)
        for d in range(1, 8):
            p = NEAR.index(8 - d)
            send(mine, wb.at[core, x, p], w2 + p, on_z(rem(z + d, 8)))

    loads[0].wait()

    @tiles
    def _(c):
        v = glu[:, lanes_of(c)].astype(f32)
        sg = jax.nn.sigmoid(glu[:, lanes_of(c, CH)].astype(f32))
        u = (live() * v * sg).astype(bf16)
        hs[0, :, lanes_of(c)] = u[:REACH]
        hs[1, :, lanes_of(c)] = u[ROWS - REACH:]
        ub[pl.ds(REACH, ROWS), lanes_of(c)] = u
        unit[c, pl.ds(REACH, ROWS), :] = u.astype(f32)

    @pl.when(ctx == 0)
    def _():
        hr[0] = jnp.zeros((REACH, CH), bf16)
        dr_[0] = jnp.zeros((REACH, CH), bf16)

    @pl.when(ctx == 7)
    def _():
        hr[1] = jnp.zeros((REACH, CH), bf16)
        dr_[1] = jnp.zeros((REACH, CH), bf16)


    def halo(src, dst):
        base = rsems(2)
        to_left = copy(src.at[0], dst.at[1], base + 1, (dp, ctx - 1))
        to_right = copy(src.at[1], dst.at[0], base, (dp, ctx + 1))

        @pl.when(ctx > 0)
        def _():
            to_left.start()

        @pl.when(ctx < 7)
        def _():
            to_right.start()

        def done():
            @pl.when(ctx > 0)
            def _():
                arrived(dst.at[0], base)
                to_left.wait_send()

            @pl.when(ctx < 7)
            def _():
                arrived(dst.at[1], base + 1)
                to_right.wait_send()

        return done

    halo_done = halo(hs, hr)

    halo_done()
    for c in (loads[1], loads[3], loads[4]):
        c.wait()
    stat[6:7] = gain_v[...].reshape(1, CH)
    stat[7:8] = bias_v[...].reshape(1, CH)
    ub[pl.ds(0, REACH), :] = hr[0]
    ub[pl.ds(REACH + ROWS, REACH), :] = hr[1]

    @tiles
    def _(c):
        unit[c, pl.ds(0, REACH), :] = hr[0, :, lanes_of(c)].astype(f32)
        unit[c, pl.ds(REACH + ROWS, REACH), :] = hr[1, :, lanes_of(c)].astype(f32)
        acc = jnp.zeros((ROWS, LANES), f32)
        for k in range(TAPS):
            acc = acc + kern[pl.ds(k, 1), lanes_of(c)] * unit[c, pl.ds(k + 1, ROWS), :]
        conv[c] = acc
        m = live()
        s = jnp.sum(m * acc, 0, keepdims=True)
        centred = acc - s / jnp.maximum(n_live, 1.0)
        q = jnp.sum(m * centred * centred, 0, keepdims=True)
        a1[g, :, lanes_of(c)] = jnp.concatenate([s, q], 0)

    a1[g, :, pl.ds(CH, LANES)] = jnp.full((2, LANES), n_live, f32)

    def merged(buf):
        total = buf[0]
        for i in range(1, 8):
            total = total + buf[i]
        s, q, n = total[0:1, 0:CH], total[1:2, 0:CH], total[0:1, CH:]
        mean = s / jnp.maximum(jnp.concatenate([n] * TILES, 1), 1.0)
        for i in range(8):
            n_i = buf[i, 0:1, CH:]
            r_i = 1.0 / jnp.maximum(n_i, 1.0)
            off = buf[i, 0:1, 0:CH] - jnp.concatenate([n_i] * TILES, 1) * mean
            q = q + off * off * jnp.concatenate([r_i] * TILES, 1)
        return s, q, n

    def packed(s, q, n):
        return jnp.concatenate([jnp.concatenate([s, n], 1), jnp.concatenate([q, n], 1)], 0)

    def summed(buf):
        total = buf[0]
        for i in range(1, 8):
            total = total + buf[i]
        return total

    a_done = exchange(a1, g, on_g)

    w1_done()

    n_rows = jnp.clip(length - pos0, 0, ROWS)
    tap = lax.broadcasted_iota(jnp.int32, (32, ROWS + 2 * REACH), 0)
    row = lax.broadcasted_iota(jnp.int32, (32, ROWS + 2 * REACH), 1) - tap - 1
    window = ((row >= 0) & (row < n_rows) & (tap < TAPS)).astype(f32).astype(bf16)
    u_sum = jnp.dot(window, ub[...], preferred_element_type=f32)
    for j in range(8):
        uq[j, 0:4, :] = u_sum[4 * j:4 * j + 4]

    @tiles
    def _(c):
        at = lanes_of(c)
        d = live() * conv[c]
        for k in range(TAPS):
            uq[k // 4, pl.ds(4 + k % 4, 1), at] = jnp.sum(d * unit[c, pl.ds(k + 1, ROWS), :], 0, keepdims=True)
        uq[7, 7:8, at] = jnp.zeros((1, LANES), f32)

    a_done()
    a2[y] = packed(*merged(a1))
    a_done = exchange(a2, y, on_y)

    groups = ((0, 5), (5, 3))

    def onward(i):
        first, size = groups[i]
        for p in range(max(first, 1), first + size):
            arrived(wb.at[core, x, p], w2 + p)
        strip = wb.at[core, x, pl.ds(first, size)]
        for d in range(1, 4):
            send(strip, strip, w3 + 4 * i + d, on_x(rem(x + d, 4)))
        send(strip, strip, w4 + 4 * i, sibling)

    def across(i):
        first, size = groups[i]
        for d in range(1, 4):
            piece = wb.at[core, rem(x + (4 - d), 4), pl.ds(first, size)]
            arrived(piece, w3 + 4 * i + d)
            send(piece, piece, w4 + 4 * i + d, sibling)

    onward(0)
    a_done()
    a3[z] = packed(*merged(a2))
    a_done = exchange(a3, z, on_z)
    onward(1)
    across(0)
    a_done()
    s, q, n = merged(a3)
    n = jnp.concatenate([n] * TILES, 1)
    stat[0:1] = s / n
    stat[1:2] = lax.rsqrt(q / n + eps)
    stat[2:3] = 1.0 / n
    stat[3:4] = lax.rsqrt(n)

    @tiles
    def _(c):
        at = lanes_of(c)
        normed = (conv[c] - stat[0:1, at]) * stat[1:2, at]
        conv[c] = normed
        pre = stat[6:7, at] * normed + stat[7:8, at]
        sp = jax.nn.sigmoid(pre)
        m = live()
        act[:, at] = (m * pre * sp).astype(bf16)
        fac[c] = m * sp * (1.0 + pre * (1.0 - sp))

    across(1)
    uq1 = rsems(8)
    for d in range(1, 8):
        j = rem(g + d, 8)
        send(uq.at[j], ur.at[d], uq1 + d, on_g(j))
    for i, (first, size) in enumerate(groups):
        for d in range(4):
            arrived(wb.at[sib, rem(x + (4 - d), 4), pl.ds(first, size)], w4 + 4 * i + d)
    for p in range(NZ):
        rows = pl.ds(pl.multiple_of(rem(z + NEAR[p], 8) * 96, 16), 96)
        for h in range(2):
            wfull[h, rows, :] = wb[h, :, p].astype(f32).reshape(96, HALF).astype(bf16)
    loads[2].wait()
    nt = (((1,), (1,)), ((), ()))
    da[...] = (lax.dot_general(cot[:, 0:HALF], wfull[0], nt, preferred_element_type=f32)
               + lax.dot_general(cot[:, HALF:CH], wfull[1], nt, preferred_element_type=f32))

    @tiles
    def _(c):
        at = lanes_of(c)
        d_pre = da[:, at] * fac[c]
        fac[c] = d_pre
        b1[g, :, at] = jnp.concatenate(
            [jnp.sum(d_pre, 0, keepdims=True), jnp.sum(d_pre * conv[c], 0, keepdims=True)], 0)

    b_done = exchange(b1, g, on_g)

    tn = (((0,), (0,)), ((), ()))

    gc, gx, gy = rsems(CHUNKS), rsems(4 * CHUNKS), rsems(8 * CHUNKS)

    @tiles
    def _(c):
        at = lanes_of(c)
        rows = pl.ds(pl.multiple_of(c * LANES, LANES), LANES)
        a = act[:, at]
        g_sib = lax.dot_general(a, cot[:, sib_cols], tn, preferred_element_type=f32).astype(bf16)
        g_own = lax.dot_general(a, cot[:, own_cols], tn, preferred_element_type=f32)
        for q in range(CHUNKS):
            gsend[q, rows, :] = g_sib[:, q * LANES:(q + 1) * LANES]
            gown[q, rows, :] = g_own[:, q * LANES:(q + 1) * LANES]
        d = fac[c]
        for k in range(TAPS):
            kt[k // 4, pl.ds(k % 4, 1), at] = jnp.sum(d * unit[c, pl.ds(k + 1, ROWS), :], 0, keepdims=True)
        kt[7, 3:4, at] = jnp.zeros((1, LANES), f32)

    for q in range(CHUNKS):
        send(gsend.at[q], grc.at[q], gc + q, sibling)
    k1 = rsems(8)
    for d in range(1, 8):
        j = rem(g + d, 8)
        send(kt.at[j], kr.at[d], k1 + d, on_g(j))
    b_done()
    b2[y] = summed(b1)
    b_done = exchange(b2, y, on_y)
    for d in range(1, 8):
        arrived(ur.at[d], uq1 + d)
    t = uq[g]
    for d in range(1, 8):
        t = t + ur[d]
    u2[y] = t
    u_done = exchange(u2, y, on_y)

    for q in range(CHUNKS):
        arrived(grc.at[q], gc + q)
        t = gown[q] + grc[q].astype(f32)
        gown[q] = t
        gxs[q] = t.astype(bf16).reshape(NX, 192, LANES)
        for d in range(1, 4):
            j = rem(x + d, 4)
            send(gxs.at[q, j], gxr.at[q, d], gx + 4 * q + d, on_x(j))

    b_done()
    b3[z] = summed(b2)
    b_done = exchange(b3, z, on_z)

    def x_part(q):
        for d in range(1, 4):
            arrived(gxr.at[q, d], gx + 4 * q + d)
        t = gown[q, pl.ds(pl.multiple_of(x * 192, 16), 192), :]
        for d in range(1, 4):
            t = t + gxr[q, d].astype(f32)
        t = t.reshape(24, 8, LANES)
        gyf[q] = t
        gys[q] = t.astype(bf16)
        for d in range(1, 8):
            j = rem(y + d, 8)
            send(gys.at[q, pl.ds(rem(j, 2) * 12 + div(j, 2) * 3, 3)], gyr.at[q, d], gy + 8 * q + d, on_y(j))

    for d in range(1, 8):
        arrived(kr.at[d], k1 + d)
    t = kt[g]
    for d in range(1, 8):
        t = t + kr[d]
    k2[y] = t
    k_done = exchange(k2, y, on_y)
    x_part(0)
    for h in range(2):
        out[:, h * HALF:(h + 1) * HALF] = jnp.dot(act[...], wfull[h], preferred_element_type=f32).astype(bf16)
    store_out = pltpu.make_async_copy(out, out_hbm, lsem.at[6])
    store_out.start()
    b_done()
    sums = summed(b3)
    gb_ref[...] = (sums[0:1] * stat[3:4]).reshape(CH)
    gn_ref[...] = (sums[1:2] * stat[3:4]).reshape(CH)
    stat[4:5] = sums[0:1] * stat[2:3]
    stat[5:6] = sums[1:2] * stat[2:3]

    @tiles
    def _(c):
        at = lanes_of(c)
        d = (live() * (stat[6:7, at] * stat[1:2, at])
             * (fac[c] - stat[4:5, at] - conv[c] * stat[5:6, at])).astype(bf16)
        ds_[0, :, at] = d[:REACH]
        ds_[1, :, at] = d[ROWS - REACH:]
        dwide[c, pl.ds(REACH, ROWS), :] = d.astype(f32)

    halo_done = halo(ds_, dr_)

    u_done()
    u_all = summed(u2)
    k_done()
    u_rows, q_rows = u_all[0:4], u_all[4:8]
    inv = stat[1:2]
    k3[z] = (stat[6:7] * inv) * (
        summed(k2) - stat[4:5] * u_rows - stat[5:6] * (inv * (q_rows - stat[0:1] * u_rows)))
    k_done = exchange(k3, z, on_z)
    x_part(1)
    x_part(2)

    owner = 2 * x + yl
    gzb = rsems(8)
    slot = rem(z + 8 - owner, 8)

    def y_part(q):
        for d in range(1, 8):
            arrived(gyr.at[q, d], gy + 8 * q + d)
        t = gyf[q, pl.ds(yl * 12 + yh * 3, 3)]
        for d in range(1, 8):
            t = t + gyr[q, d].astype(f32)
        gz[q] = t

    halo_done()

    @tiles
    def _(c):
        at = lanes_of(c)
        dwide[c, pl.ds(0, REACH), :] = dr_[0, :, at].astype(f32)
        dwide[c, pl.ds(REACH + ROWS, REACH), :] = dr_[1, :, at].astype(f32)
        acc = jnp.zeros((ROWS, LANES), f32)
        for k in range(TAPS):
            acc = acc + kern[pl.ds(k, 1), at] * dwide[c, pl.ds(TAPS - k, ROWS), :]
        v = glu[:, at].astype(f32)
        sg = jax.nn.sigmoid(glu[:, lanes_of(c, CH)].astype(f32))
        du = live() * acc * sg
        gg[:, at] = du.astype(bf16)
        gg[:, lanes_of(c, CH)] = (du * v * (1.0 - sg)).astype(bf16)

    store_gg = pltpu.make_async_copy(gg, gg_hbm, lsem.at[7])
    store_gg.start()

    for q in range(CHUNKS):
        y_part(q)
    to_owner = copy(gz, gzr.at[slot], gzb + slot, on_z(owner))
    cond.append((z != owner, [to_owner]))

    @pl.when(z != owner)
    def _():
        to_owner.start()

    k_done()
    kf[g] = summed(k3) * stat[3:4]
    k_done = exchange(kf, g, on_g)

    fbb = rsems(2)
    spread = []
    for d in range(1, 16):
        e = rem(core + d, 2)
        c_ = rem(ctx + d // 2, 8)
        spread.append(copy(fin.at[pl.ds(e, 2)], fb.at[core], fbb + core, (div(dp, 2) * 2 + e, c_)))
    cond.append((z == owner, spread))

    @pl.when(z == owner)
    def _():
        for d in range(1, 8):
            arrived(gzr.at[d], gzb + d)
        for q in range(CHUNKS):
            t = gz[q]
            for d in range(1, 8):
                t = t + gzr[d, q]
            t = t * stat[3:4, 0:LANES].reshape(1, 1, LANES)
            for u in range(3):
                fin[u, q] = t[u]
        for c in spread:
            c.start()
        fb[core] = fin[pl.ds(core, 2)]

    k_done()
    for j in range(8):
        w = 4 if j < 7 else 3
        gk_ref[pl.ds(4 * j, w), :] = kf[j, 0:w, :]

    @pl.when(z != owner)
    def _():
        arrived(fb.at[core], fbb + core)

    arrived(fb.at[sib], fbb + sib)
    for h in range(2):
        for q in range(CHUNKS):
            v = jnp.concatenate([fb[h, 0, q], fb[h, 1, q]], 0)
            gp_ref[:, pl.ds(h * HALF + q * LANES, LANES)] = jnp.where(core == 0, v[0:BLOCK], v[16 - BLOCK:16])

    finish()
    store_out.wait()
    store_gg.wait()


def handed_on(*refs):
    sem = refs[12]
    copies = [pltpu.make_async_copy(refs[i], refs[6 + i], sem.at[i]) for i in range(6)]
    for c in copies:
        c.start()
    for c in copies:
        c.wait()


def body(glu_in, lengths, kernel, bn_gain, bn_bias, proj_weight, cotangent):
    vm = pltpu.VMEM
    hbm = functools.partial(pltpu.with_memory_space_constraint, memory_space=pltpu.HBM)
    anyspec = pl.BlockSpec(memory_space=pl.ANY)
    vspec = pl.BlockSpec(memory_space=pltpu.VMEM)
    sspec = pl.BlockSpec(memory_space=pltpu.SMEM)
    scratch = [
        vm((ROWS, 2 * CH), bf16), vm((ROWS, CH), bf16), vm((TAPS, CH), f32),
        vm((TILES, ROWS + 2 * REACH, LANES), f32), vm((TILES, ROWS, LANES), f32),
        vm((TILES, ROWS, LANES), f32), vm((TILES, ROWS + 2 * REACH, LANES), f32),
        vm((ROWS, CH), f32), vm((ROWS, CH), bf16), vm((ROWS, CH), bf16), vm((ROWS, 2 * CH), bf16),
        vm((ROWS + 2 * REACH, CH), bf16),
        vm((BLOCK, CH), bf16), vm((NC, BLOCK, HALF), bf16),
        vm((NC, NYH, NZ, 3, 8, HALF), bf16), vm((NC, CH, HALF), bf16),
        vm((2, REACH, CH), bf16), vm((2, REACH, CH), bf16), vm((2, REACH, CH), bf16), vm((2, REACH, CH), bf16),
        vm((8, 2, CH + LANES), f32), vm((8, 2, CH + LANES), f32), vm((8, 2, CH + LANES), f32),
        vm((8, 2, CH), f32), vm((8, 2, CH), f32), vm((8, 2, CH), f32),
        vm((8, CH), f32),
        vm((8, 4, CH), f32), vm((8, 4, CH), f32), vm((8, 4, CH), f32), vm((8, 4, CH), f32), vm((8, 4, CH), f32),
        vm((8, 8, CH), f32), vm((8, 8, CH), f32), vm((8, 8, CH), f32),
        vm((CHUNKS, CH, LANES), f32), vm((CHUNKS, CH, LANES), bf16), vm((CHUNKS, CH, LANES), bf16),
        vm((CHUNKS, NX, 192, LANES), bf16), vm((CHUNKS, NX, 192, LANES), bf16),
        vm((CHUNKS, 24, 8, LANES), f32), vm((CHUNKS, 24, 8, LANES), bf16), vm((CHUNKS, 8, 3, 8, LANES), bf16),
        vm((CHUNKS, 3, 8, LANES), f32), vm((8, CHUNKS, 3, 8, LANES), f32),
        vm((3, CHUNKS, 8, LANES), f32), vm((2, 2, CHUNKS, 8, LANES), f32),
        vm((CH,), f32), vm((CH,), f32),
        pltpu.SemaphoreType.DMA((200,)), pltpu.SemaphoreType.DMA((200,)), pltpu.SemaphoreType.DMA((8,)),
    ]
    outs = [
        jax.ShapeDtypeStruct((ROWS, CH), bf16),
        jax.ShapeDtypeStruct((ROWS, 2 * CH), bf16),
        jax.ShapeDtypeStruct((BLOCK, CH), f32),
        jax.ShapeDtypeStruct((TAPS, CH), f32),
        jax.ShapeDtypeStruct((CH,), f32),
        jax.ShapeDtypeStruct((CH,), f32),
    ]
    results = pl.pallas_call(
        fused,
        out_shape=outs,
        in_specs=[anyspec, sspec, anyspec, anyspec, anyspec, anyspec, anyspec],
        out_specs=[anyspec, anyspec, vspec, vspec, vspec, vspec],
        scratch_shapes=scratch,
        compiler_params=pltpu.CompilerParams(
            collective_id=0, has_side_effects=True, vmem_limit_bytes=40 * 1024 * 1024),
        name="conformer_conv",
    )(hbm(glu_in[0]), lengths, hbm(kernel), hbm(bn_gain), hbm(bn_bias), hbm(proj_weight), hbm(cotangent[0]))
    result, grad_glu, grad_proj, grad_kernel, grad_gain, grad_bias = pl.pallas_call(
        handed_on,
        out_shape=outs,
        in_specs=[anyspec] * 6,
        out_specs=[anyspec] * 6,
        scratch_shapes=[pltpu.SemaphoreType.DMA((6,))],
        compiler_params=pltpu.CompilerParams(vmem_limit_bytes=1024 * 1024),
        name="handed_on",
    )(*results)
    return (result[None], grad_glu[None], grad_proj, grad_kernel, grad_gain, grad_bias)


def solution(mesh):
    in_specs = (P("dp", "ctx", None), P("dp"), P(), P(), P(), P("dp", None), P("dp", "ctx", None))
    out_specs = (P("dp", "ctx", None), P("dp", "ctx", None), P("dp", None), P(), P(), P())
    return jax.shard_map(body, mesh=mesh, in_specs=in_specs, out_specs=out_specs, check_vma=False)
```

```python
import functools

import jax
import jax.numpy as jnp
from jax import lax
from jax.experimental import pallas as pl
from jax.experimental.pallas import tpu as pltpu
from jax.sharding import PartitionSpec as P

eps = 1e-05
f32 = jnp.float32
bf16 = jnp.bfloat16

NZ, NYH, NC, NYL, NX = 8, 4, 2, 2, 4
ROWS, CH, TAPS, LANES = 128, 768, 31, 128
TILES = CH // LANES
HALF = CH // 2
REACH = 16
BLOCK = CH // (NZ * NYH * NC)
CHUNKS = HALF // LANES
NEAR = (0, 1, 7, 2, 6, 3, 5, 4)


def rem(a, b):
    return lax.rem(a, jnp.int32(b))


def div(a, b):
    return lax.div(a, jnp.int32(b))


def lanes_of(c, first=0):
    return pl.ds(pl.multiple_of(first + c * LANES, LANES), LANES)


def tiles(fn):
    def step(c, carry):
        fn(c)
        return carry

    lax.fori_loop(0, TILES, step, 0)


def fused(glu_hbm, len_ref, kern_hbm, gain_in, bias_in, w_hbm, cot_hbm,
          out_hbm, gg_hbm, gp_ref, gk_ref, gn_ref, gb_ref,
          glu, cot, kern, unit, conv, fac, dwide, da, act, out, gg, ub,
          wl, wr, wb, wfull, hs, hr, ds_, dr_, a1, a2, a3, b1, b2, b3, stat,
          kt, kr, k2, k3, kf, uq, ur, u2, gown, gsend, grc, gxs, gxr, gyf, gys, gyr, gz, gzr, fin, fb,
          hz, hzr, hy, hyr, hx, hfin, hfb,
          gain_v, bias_v, ssem, rsem, lsem):
    dp = lax.axis_index("dp")
    ctx = lax.axis_index("ctx")
    z, yh, core = div(dp, 8), rem(div(dp, 2), 4), rem(dp, 2)
    yl, x = div(ctx, 4), rem(ctx, 4)
    y = yh * 2 + yl
    g = x * 2 + core
    sib = 1 - core

    def dev(z_, y_, x_, c_):
        return (z_ * 8 + div(y_, 2) * 2 + c_, rem(y_, 2) * 4 + x_)

    def on_g(j):
        return dev(z, y, div(j, 2), rem(j, 2))

    def on_y(j):
        return dev(z, j, x, core)

    def on_z(j):
        return dev(j, y, x, core)

    def on_x(j):
        return dev(z, y, j, core)

    sibling = dev(z, y, x, sib)
    used = [0, 0]
    pending = []
    cond = []

    def ssems(n=1):
        used[0] += n
        return used[0] - n

    def rsems(n=1):
        used[1] += n
        return used[1] - n

    def desc(src, dst, ssend, recv, target):
        return pltpu.make_async_remote_copy(
            src_ref=src, dst_ref=dst, send_sem=ssem.at[ssend], recv_sem=rsem.at[recv],
            device_id=target, device_id_type=pl.DeviceIdType.MESH)

    def copy(src, dst, recv, target):
        return desc(src, dst, ssems(), recv, target)

    def send(src, dst, recv, target):
        c = copy(src, dst, recv, target)
        c.start()
        pending.append(c)

    def group(copies, total, recv):
        sem = ssems()
        for src, dst, target in copies:
            desc(src, dst, sem, recv, target).start()
        pending.append(desc(total, total, sem, recv, sibling))

    def arrived(dst, recv):
        desc(dst, dst, 0, recv, sibling).wait_recv()

    def finish():
        for c in pending:
            c.wait_send()
        for when, copies in cond:
            @pl.when(when)
            def _():
                for c in copies:
                    c.wait_send()

    def exchange(buf, me, where, n=8):
        recv = rsems()
        others = buf.at[pl.ds(0, n - 1)]
        group([(buf.at[me], buf.at[me], where(rem(me + d, n))) for d in range(1, n)], others, recv)
        return lambda: arrived(others, recv)

    def scatter(src_of, dst_of, total_src, total_dst, me, where, n=8):
        recv = rsems()
        copies = []
        for d in range(1, n):
            j = rem(me + d, n)
            copies.append((src_of(j), dst_of(d), where(j)))
        group(copies, total_src, recv)
        return lambda: arrived(total_dst, recv)

    barrier = pltpu.get_barrier_semaphore()
    peers = [on_g(rem(g + d, 8)) for d in range(1, 8)]
    peers += [on_y(rem(y + d, 8)) for d in range(1, 8)]
    peers += [on_z(rem(z + d, 8)) for d in range(1, 8)]
    flip = yh * 2 + (1 - yl)
    peers += [dev(z, rem(y + 2 * d, 8), x, sib) for d in range(1, 4)]
    peers += [dev(z, flip, div(rem(g + d, 8), 2), rem(rem(g + d, 8), 2)) for d in range(1, 8)]
    for p in peers:
        pl.semaphore_signal(barrier, inc=1, device_id=p, device_id_type=pl.DeviceIdType.MESH)

    loads = [pltpu.make_async_copy(a, b, lsem.at[i]) for i, (a, b) in enumerate(
        [(glu_hbm, glu), (kern_hbm, kern), (cot_hbm, cot), (gain_in, gain_v), (bias_in, bias_v)])]
    load_w = pltpu.make_async_copy(w_hbm, wl, lsem.at[5])

    @pl.when(yh == x)
    def _():
        load_w.start()

    for c in loads:
        c.start()

    pos0 = ctx * ROWS
    length = len_ref[0]
    n_live = jnp.clip(length - pos0, 0, ROWS).astype(f32)

    def live():
        return (lax.broadcasted_iota(jnp.int32, (ROWS, LANES), 0) + pos0 < length).astype(f32)

    pl.semaphore_wait(barrier, len(peers))

    own_cols = pl.ds(pl.multiple_of(core * HALF, LANES), HALF)
    sib_cols = pl.ds(pl.multiple_of(sib * HALF, LANES), HALF)
    w1, w2, w3, w4 = rsems(2), rsems(2), rsems(8), rsems(2)
    mine = wb.at[core, x, 0]
    groups = ((0, 5), (5, 3))
    w4_sems = []
    w1_sends = [copy(wl.at[:, sib_cols], wr.at[core], w1 + core, sibling)]
    for d in range(1, 4):
        y_ = rem(yh + d, 4) * 2 + yl
        w1_sends.append(copy(wl.at[:, own_cols], wr.at[core], w1 + core, dev(z, y_, x, core)))
        w1_sends.append(copy(wl.at[:, sib_cols], wr.at[core], w1 + core, dev(z, y_, x, sib)))
    cond.append((yh == x, w1_sends))

    @pl.when(yh == x)
    def _():
        load_w.wait()
        for c in w1_sends:
            c.start()
        wr[core] = wl[:, own_cols]

    def w1_done():
        @pl.when(yh != x)
        def _():
            arrived(wr.at[core], w1 + core)

        arrived(wr.at[sib], w1 + sib)
        rows = jnp.concatenate([wr[0].astype(f32), wr[1].astype(f32)], 0)
        wb[core, x, 0] = rows.reshape(3, 8, HALF).astype(bf16)
        for i, (first, size) in enumerate(groups):
            places = range(max(first, 1), first + size)
            group([(mine, wb.at[core, x, p], on_z(rem(z + 8 - NEAR[p], 8))) for p in places],
                  wb.at[core, x, pl.ds(places[0], len(places))], w2 + i)

    loads[0].wait()

    @tiles
    def _(c):
        v = glu[:, lanes_of(c)].astype(f32)
        sg = jax.nn.sigmoid(glu[:, lanes_of(c, CH)].astype(f32))
        u = (live() * v * sg).astype(bf16)
        hs[0, :, lanes_of(c)] = u[:REACH]
        hs[1, :, lanes_of(c)] = u[ROWS - REACH:]
        ub[pl.ds(REACH, ROWS), lanes_of(c)] = u
        unit[c, pl.ds(REACH, ROWS), :] = u.astype(f32)

    @pl.when(ctx == 0)
    def _():
        hr[0] = jnp.zeros((REACH, CH), bf16)
        dr_[0] = jnp.zeros((REACH, CH), bf16)

    @pl.when(ctx == 7)
    def _():
        hr[1] = jnp.zeros((REACH, CH), bf16)
        dr_[1] = jnp.zeros((REACH, CH), bf16)


    def halo(src, dst):
        base = rsems(2)
        to_left = copy(src.at[0], dst.at[1], base + 1, (dp, ctx - 1))
        to_right = copy(src.at[1], dst.at[0], base, (dp, ctx + 1))

        @pl.when(ctx > 0)
        def _():
            to_left.start()

        @pl.when(ctx < 7)
        def _():
            to_right.start()

        def done():
            @pl.when(ctx > 0)
            def _():
                arrived(dst.at[0], base)
                to_left.wait_send()

            @pl.when(ctx < 7)
            def _():
                arrived(dst.at[1], base + 1)
                to_right.wait_send()

        return done

    halo_done = halo(hs, hr)

    halo_done()
    for c in (loads[1], loads[3], loads[4]):
        c.wait()
    stat[6:7] = gain_v[...].reshape(1, CH)
    stat[7:8] = bias_v[...].reshape(1, CH)
    ub[pl.ds(0, REACH), :] = hr[0]
    ub[pl.ds(REACH + ROWS, REACH), :] = hr[1]

    @tiles
    def _(c):
        unit[c, pl.ds(0, REACH), :] = hr[0, :, lanes_of(c)].astype(f32)
        unit[c, pl.ds(REACH + ROWS, REACH), :] = hr[1, :, lanes_of(c)].astype(f32)
        acc = jnp.zeros((ROWS, LANES), f32)
        for k in range(TAPS):
            acc = acc + kern[pl.ds(k, 1), lanes_of(c)] * unit[c, pl.ds(k + 1, ROWS), :]
        conv[c] = acc
        m = live()
        s = jnp.sum(m * acc, 0, keepdims=True)
        centred = acc - s / jnp.maximum(n_live, 1.0)
        q = jnp.sum(m * centred * centred, 0, keepdims=True)
        a1[g, :, lanes_of(c)] = jnp.concatenate([s, q], 0)

    a1[g, :, pl.ds(CH, LANES)] = jnp.full((2, LANES), n_live, f32)

    def merged(buf):
        total = buf[0]
        for i in range(1, 8):
            total = total + buf[i]
        s, q, n = total[0:1, 0:CH], total[1:2, 0:CH], total[0:1, CH:]
        mean = s / jnp.maximum(jnp.concatenate([n] * TILES, 1), 1.0)
        for i in range(8):
            n_i = buf[i, 0:1, CH:]
            r_i = 1.0 / jnp.maximum(n_i, 1.0)
            off = buf[i, 0:1, 0:CH] - jnp.concatenate([n_i] * TILES, 1) * mean
            q = q + off * off * jnp.concatenate([r_i] * TILES, 1)
        return s, q, n

    def packed(s, q, n):
        return jnp.concatenate([jnp.concatenate([s, n], 1), jnp.concatenate([q, n], 1)], 0)

    def summed(buf):
        total = buf[0]
        for i in range(1, 8):
            total = total + buf[i]
        return total

    a_done = exchange(a1, g, on_g)

    w1_done()

    n_rows = jnp.clip(length - pos0, 0, ROWS)
    tap = lax.broadcasted_iota(jnp.int32, (32, ROWS + 2 * REACH), 0)
    row = lax.broadcasted_iota(jnp.int32, (32, ROWS + 2 * REACH), 1) - tap - 1
    window = ((row >= 0) & (row < n_rows) & (tap < TAPS)).astype(f32).astype(bf16)
    u_sum = jnp.dot(window, ub[...], preferred_element_type=f32)
    for j in range(8):
        uq[j, 0:4, :] = u_sum[4 * j:4 * j + 4]

    @tiles
    def _(c):
        at = lanes_of(c)
        d = live() * conv[c]
        for k in range(TAPS):
            uq[k // 4, pl.ds(4 + k % 4, 1), at] = jnp.sum(d * unit[c, pl.ds(k + 1, ROWS), :], 0, keepdims=True)
        uq[7, 7:8, at] = jnp.zeros((1, LANES), f32)

    a_done()
    a2[y] = packed(*merged(a1))
    a_done = exchange(a2, y, on_y)

    def onward(i):
        first, size = groups[i]
        some = max(first, 1)
        arrived(wb.at[core, x, pl.ds(some, first + size - some)], w2 + i)
        strip = wb.at[core, x, pl.ds(first, size)]
        sem = ssems()
        for d in range(1, 4):
            desc(strip, strip, sem, w3 + 4 * i + d, on_x(rem(x + d, 4))).start()
        pending.append(desc(wb.at[core, pl.ds(0, 3), pl.ds(first, size)],
                            wb.at[core, pl.ds(0, 3), pl.ds(first, size)], sem, 0, sibling))
        w4_sems.append(ssems())
        desc(strip, strip, w4_sems[i], w4 + i, sibling).start()

    def across(i):
        first, size = groups[i]
        for d in range(1, 4):
            piece = wb.at[core, rem(x + (4 - d), 4), pl.ds(first, size)]
            arrived(piece, w3 + 4 * i + d)
            desc(piece, piece, w4_sems[i], w4 + i, sibling).start()
        whole = wb.at[core, :, pl.ds(first, size)]
        pending.append(desc(whole, whole, w4_sems[i], 0, sibling))

    onward(0)
    a_done()
    a3[z] = packed(*merged(a2))
    a_done = exchange(a3, z, on_z)
    onward(1)
    uq_done = scatter(lambda j: uq.at[j], lambda d: ur.at[d], uq.at[pl.ds(0, 7)], ur.at[pl.ds(1, 7)], g, on_g)
    across(0)
    a_done()
    s, q, n = merged(a3)
    n = jnp.concatenate([n] * TILES, 1)
    stat[0:1] = s / n
    stat[1:2] = lax.rsqrt(q / n + eps)
    stat[2:3] = 1.0 / n
    stat[3:4] = lax.rsqrt(n)

    @tiles
    def _(c):
        at = lanes_of(c)
        normed = (conv[c] - stat[0:1, at]) * stat[1:2, at]
        conv[c] = normed
        pre = stat[6:7, at] * normed + stat[7:8, at]
        sp = jax.nn.sigmoid(pre)
        m = live()
        act[:, at] = (m * pre * sp).astype(bf16)
        fac[c] = m * sp * (1.0 + pre * (1.0 - sp))

    across(1)
    uq_done()
    t = uq[g]
    for d in range(1, 8):
        t = t + ur[d]
    u2[y] = t
    u_done = exchange(u2, y, on_y)
    for i, (first, size) in enumerate(groups):
        arrived(wb.at[sib, :, pl.ds(first, size)], w4 + i)
    for p in range(NZ):
        rows = pl.ds(pl.multiple_of(rem(z + NEAR[p], 8) * 96, 16), 96)
        for h in range(2):
            wfull[h, rows, :] = wb[h, :, p].astype(f32).reshape(96, HALF).astype(bf16)
    loads[2].wait()
    nt = (((1,), (1,)), ((), ()))
    da[...] = (lax.dot_general(cot[:, 0:HALF], wfull[0], nt, preferred_element_type=f32)
               + lax.dot_general(cot[:, HALF:CH], wfull[1], nt, preferred_element_type=f32))

    @tiles
    def _(c):
        at = lanes_of(c)
        d_pre = da[:, at] * fac[c]
        fac[c] = d_pre
        b1[g, :, at] = jnp.concatenate(
            [jnp.sum(d_pre, 0, keepdims=True), jnp.sum(d_pre * conv[c], 0, keepdims=True)], 0)

    b_done = exchange(b1, g, on_g)

    tn = (((0,), (0,)), ((), ()))

    gc, h3 = rsems(CHUNKS), rsems(CHUNKS)
    h1_done, h2_done = {}, {}

    @tiles
    def _(c):
        at = lanes_of(c)
        rows = pl.ds(pl.multiple_of(c * LANES, LANES), LANES)
        a = act[:, at]
        g_sib = lax.dot_general(a, cot[:, sib_cols], tn, preferred_element_type=f32).astype(bf16)
        g_own = lax.dot_general(a, cot[:, own_cols], tn, preferred_element_type=f32)
        for q in range(CHUNKS):
            gsend[q, rows, :] = g_sib[:, q * LANES:(q + 1) * LANES]
            gown[q, rows, :] = g_own[:, q * LANES:(q + 1) * LANES]
        d = fac[c]
        for k in range(TAPS):
            kt[k // 4, pl.ds(k % 4, 1), at] = jnp.sum(d * unit[c, pl.ds(k + 1, ROWS), :], 0, keepdims=True)
        kt[7, 3:4, at] = jnp.zeros((1, LANES), f32)

    for q in (1, 2, 0):
        send(gsend.at[q], grc.at[q], gc + q, sibling)
    k1_done = scatter(lambda j: kt.at[j], lambda d: kr.at[d], kt.at[pl.ds(0, 7)], kr.at[pl.ds(1, 7)], g, on_g)
    b_done()
    b2[z] = summed(b1)
    b_done = exchange(b2, z, on_z)

    for q in (1, 2, 0):
        arrived(grc.at[q], gc + q)
        t = gown[q] + grc[q].astype(f32)
        gown[q] = t
        if q == 0:
            gxs[...] = t.astype(bf16).reshape(NX, 192, LANES)
            gx_done = scatter(lambda j: gxs.at[j], lambda d: gxr.at[d],
                              gxs.at[pl.ds(0, 3)], gxr.at[pl.ds(1, 3)], x, on_x, NX)
        else:
            hz[q] = t.astype(bf16).reshape(NZ, 96, LANES)
            h1_done[q] = scatter(lambda j: hz.at[q, j], lambda d: hzr.at[q, d],
                                 hz.at[q, pl.ds(0, 7)], hzr.at[q, pl.ds(1, 7)], z, on_z)

    b_done()
    b3[y] = summed(b2)
    b_done = exchange(b3, y, on_y)

    def x_part():
        gx_done()
        t = gown[0, pl.ds(pl.multiple_of(x * 192, 16), 192), :]
        for d in range(1, 4):
            t = t + gxr[d].astype(f32)
        t = t.reshape(24, 8, LANES)
        gyf[...] = t
        gys[...] = t.astype(bf16)
        return scatter(lambda j: gys.at[pl.ds(rem(j, 2) * 12 + div(j, 2) * 3, 3)], lambda d: gyr.at[d],
                       gyr.at[pl.ds(0, 7)], gyr.at[pl.ds(1, 7)], y, on_y)

    def z_part(q):
        h1_done[q]()
        t = gown[q, pl.ds(pl.multiple_of(z * 96, 16), 96), :]
        for d in range(1, 8):
            t = t + hzr[q, d].astype(f32)
        hy[q] = t.reshape(12, 8, LANES).astype(bf16)
        h2_done[q] = scatter(lambda j: hy.at[q, pl.ds(div(j, 2) * 3, 3)], lambda d: hyr.at[q, y],
                             hyr.at[q, pl.ds(0, 7)], hyr.at[q, pl.ds(0, 7)], y, on_y)
        hyr[q, y] = hy[q, pl.ds(yh * 3, 3)]

    def zy_part(q):
        h2_done[q]()
        t = hyr[q, 0].astype(f32)
        for i in range(1, 8):
            t = t + hyr[q, i].astype(f32)
        hx[q, x] = t
        return exchange(hx.at[q], x, on_x, NX)

    def zyx_part(q, done):
        done()
        t = hx[q, 0]
        for i in range(1, NX):
            t = t + hx[q, i]
        hfin[q] = t * stat[3:4, 0:LANES].reshape(1, 1, LANES)
        send(hfin.at[q, pl.ds(sib, 2)], hfb.at[core, q], h3 + q, sibling)
        hfb[core, q] = hfin[q, pl.ds(core, 2)]

    k1_done()
    t = kt[g]
    for d in range(1, 8):
        t = t + kr[d]
    k2[y] = t
    k_done = exchange(k2, y, on_y)
    gy_done = x_part()
    for h in range(2):
        out[:, h * HALF:(h + 1) * HALF] = jnp.dot(act[...], wfull[h], preferred_element_type=f32).astype(bf16)
    store_out = pltpu.make_async_copy(out, out_hbm, lsem.at[6])
    store_out.start()
    b_done()
    sums = summed(b3)
    gb_ref[...] = (sums[0:1] * stat[3:4]).reshape(CH)
    gn_ref[...] = (sums[1:2] * stat[3:4]).reshape(CH)
    stat[4:5] = sums[0:1] * stat[2:3]
    stat[5:6] = sums[1:2] * stat[2:3]

    @tiles
    def _(c):
        at = lanes_of(c)
        d = (live() * (stat[6:7, at] * stat[1:2, at])
             * (fac[c] - stat[4:5, at] - conv[c] * stat[5:6, at])).astype(bf16)
        ds_[0, :, at] = d[:REACH]
        ds_[1, :, at] = d[ROWS - REACH:]
        dwide[c, pl.ds(REACH, ROWS), :] = d.astype(f32)

    halo_done = halo(ds_, dr_)

    u_done()
    u_all = summed(u2)
    k_done()
    u_rows, q_rows = u_all[0:4], u_all[4:8]
    inv = stat[1:2]
    k3[z] = (stat[6:7] * inv) * (
        summed(k2) - stat[4:5] * u_rows - stat[5:6] * (inv * (q_rows - stat[0:1] * u_rows)))
    k_done = exchange(k3, z, on_z)
    z_part(1)
    z_part(2)

    owner = 2 * x + yl
    gzb = rsems()
    slot = rem(z + 8 - owner, 8)

    def y_part():
        gy_done()
        t = gyf[pl.ds(yl * 12 + yh * 3, 3)]
        for d in range(1, 8):
            t = t + gyr[d].astype(f32)
        gz[...] = t

    y_part()
    to_owner = copy(gz, gzr.at[slot], gzb, on_z(owner))
    cond.append((z != owner, [to_owner]))

    @pl.when(z != owner)
    def _():
        to_owner.start()

    halo_done()

    @tiles
    def _(c):
        at = lanes_of(c)
        dwide[c, pl.ds(0, REACH), :] = dr_[0, :, at].astype(f32)
        dwide[c, pl.ds(REACH + ROWS, REACH), :] = dr_[1, :, at].astype(f32)
        acc = jnp.zeros((ROWS, LANES), f32)
        for k in range(TAPS):
            acc = acc + kern[pl.ds(k, 1), at] * dwide[c, pl.ds(TAPS - k, ROWS), :]
        v = glu[:, at].astype(f32)
        sg = jax.nn.sigmoid(glu[:, lanes_of(c, CH)].astype(f32))
        du = live() * acc * sg
        gg[:, at] = du.astype(bf16)
        gg[:, lanes_of(c, CH)] = (du * v * (1.0 - sg)).astype(bf16)

    store_gg = pltpu.make_async_copy(gg, gg_hbm, lsem.at[7])
    store_gg.start()

    x1_done = zy_part(1)
    k_done()
    kf[g] = summed(k3) * stat[3:4]
    k_done = exchange(kf, g, on_g)
    x2_done = zy_part(2)
    zyx_part(1, x1_done)

    fbb = rsems(2)
    spread = []
    for d in range(1, 16):
        e = rem(core + d, 2)
        c_ = rem(ctx + d // 2, 8)
        spread.append(copy(fin.at[pl.ds(e, 2)], fb.at[core], fbb + core, (div(dp, 2) * 2 + e, c_)))
    cond.append((z == owner, spread))

    @pl.when(z == owner)
    def _():
        arrived(gzr.at[pl.ds(1, 7)], gzb)
        t = gz[...]
        for d in range(1, 8):
            t = t + gzr[d]
        fin[...] = t * stat[3:4, 0:LANES].reshape(1, 1, LANES)
        for c in spread:
            c.start()
        fb[core] = fin[pl.ds(core, 2)]

    zyx_part(2, x2_done)
    k_done()
    for j in range(8):
        w = 4 if j < 7 else 3
        gk_ref[pl.ds(4 * j, w), :] = kf[j, 0:w, :]

    @pl.when(z != owner)
    def _():
        arrived(fb.at[core], fbb + core)

    arrived(fb.at[sib], fbb + sib)
    for q in (1, 2):
        arrived(hfb.at[sib, q], h3 + q)
    for h in range(2):
        for q in range(CHUNKS):
            v = fb[h] if q == 0 else hfb[h, q]
            v = v.reshape(16, LANES)
            gp_ref[:, pl.ds(h * HALF + q * LANES, LANES)] = jnp.where(core == 0, v[0:BLOCK], v[16 - BLOCK:16])

    finish()
    store_out.wait()
    store_gg.wait()


def handed_on(*refs):
    sem = refs[12]
    copies = [pltpu.make_async_copy(refs[i], refs[6 + i], sem.at[i]) for i in range(6)]
    for c in copies:
        c.start()
    for c in copies:
        c.wait()


def body(glu_in, lengths, kernel, bn_gain, bn_bias, proj_weight, cotangent):
    vm = pltpu.VMEM
    hbm = functools.partial(pltpu.with_memory_space_constraint, memory_space=pltpu.HBM)
    anyspec = pl.BlockSpec(memory_space=pl.ANY)
    vspec = pl.BlockSpec(memory_space=pltpu.VMEM)
    sspec = pl.BlockSpec(memory_space=pltpu.SMEM)
    scratch = [
        vm((ROWS, 2 * CH), bf16), vm((ROWS, CH), bf16), vm((TAPS, CH), f32),
        vm((TILES, ROWS + 2 * REACH, LANES), f32), vm((TILES, ROWS, LANES), f32),
        vm((TILES, ROWS, LANES), f32), vm((TILES, ROWS + 2 * REACH, LANES), f32),
        vm((ROWS, CH), f32), vm((ROWS, CH), bf16), vm((ROWS, CH), bf16), vm((ROWS, 2 * CH), bf16),
        vm((ROWS + 2 * REACH, CH), bf16),
        vm((BLOCK, CH), bf16), vm((NC, BLOCK, HALF), bf16),
        vm((NC, NYH, NZ, 3, 8, HALF), bf16), vm((NC, CH, HALF), bf16),
        vm((2, REACH, CH), bf16), vm((2, REACH, CH), bf16), vm((2, REACH, CH), bf16), vm((2, REACH, CH), bf16),
        vm((8, 2, CH + LANES), f32), vm((8, 2, CH + LANES), f32), vm((8, 2, CH + LANES), f32),
        vm((8, 2, CH), f32), vm((8, 2, CH), f32), vm((8, 2, CH), f32),
        vm((8, CH), f32),
        vm((8, 4, CH), f32), vm((8, 4, CH), f32), vm((8, 4, CH), f32), vm((8, 4, CH), f32), vm((8, 4, CH), f32),
        vm((8, 8, CH), f32), vm((8, 8, CH), f32), vm((8, 8, CH), f32),
        vm((CHUNKS, CH, LANES), f32), vm((CHUNKS, CH, LANES), bf16), vm((CHUNKS, CH, LANES), bf16),
        vm((NX, 192, LANES), bf16), vm((NX, 192, LANES), bf16),
        vm((24, 8, LANES), f32), vm((24, 8, LANES), bf16), vm((8, 3, 8, LANES), bf16),
        vm((3, 8, LANES), f32), vm((8, 3, 8, LANES), f32),
        vm((3, 8, LANES), f32), vm((2, 2, 8, LANES), f32),
        vm((CHUNKS, NZ, 96, LANES), bf16), vm((CHUNKS, NZ, 96, LANES), bf16),
        vm((CHUNKS, 12, 8, LANES), bf16), vm((CHUNKS, 8, 3, 8, LANES), bf16),
        vm((CHUNKS, NX, 3, 8, LANES), f32), vm((CHUNKS, 3, 8, LANES), f32), vm((2, CHUNKS, 2, 8, LANES), f32),
        vm((CH,), f32), vm((CH,), f32),
        pltpu.SemaphoreType.DMA((64,)), pltpu.SemaphoreType.DMA((64,)), pltpu.SemaphoreType.DMA((8,)),
    ]
    outs = [
        jax.ShapeDtypeStruct((ROWS, CH), bf16),
        jax.ShapeDtypeStruct((ROWS, 2 * CH), bf16),
        jax.ShapeDtypeStruct((BLOCK, CH), f32),
        jax.ShapeDtypeStruct((TAPS, CH), f32),
        jax.ShapeDtypeStruct((CH,), f32),
        jax.ShapeDtypeStruct((CH,), f32),
    ]
    results = pl.pallas_call(
        fused,
        out_shape=outs,
        in_specs=[anyspec, sspec, anyspec, anyspec, anyspec, anyspec, anyspec],
        out_specs=[anyspec, anyspec, vspec, vspec, vspec, vspec],
        scratch_shapes=scratch,
        compiler_params=pltpu.CompilerParams(
            collective_id=0, has_side_effects=True, vmem_limit_bytes=40 * 1024 * 1024),
        name="conformer_conv",
    )(hbm(glu_in[0]), lengths, hbm(kernel), hbm(bn_gain), hbm(bn_bias), hbm(proj_weight), hbm(cotangent[0]))
    result, grad_glu, grad_proj, grad_kernel, grad_gain, grad_bias = pl.pallas_call(
        handed_on,
        out_shape=outs,
        in_specs=[anyspec] * 6,
        out_specs=[anyspec] * 6,
        scratch_shapes=[pltpu.SemaphoreType.DMA((6,))],
        compiler_params=pltpu.CompilerParams(vmem_limit_bytes=1024 * 1024),
        name="handed_on",
    )(*results)
    return (result[None], grad_glu[None], grad_proj, grad_kernel, grad_gain, grad_bias)


def solution(mesh):
    in_specs = (P("dp", "ctx", None), P("dp"), P(), P(), P(), P("dp", None), P("dp", "ctx", None))
    out_specs = (P("dp", "ctx", None), P("dp", "ctx", None), P("dp", None), P(), P(), P())
    return jax.shard_map(body, mesh=mesh, in_specs=in_specs, out_specs=out_specs, check_vma=False)
```

```python
import functools

import jax
import jax.numpy as jnp
from jax import lax
from jax.experimental import pallas as pl
from jax.experimental.pallas import tpu as pltpu
from jax.sharding import PartitionSpec as P

eps = 1e-05
f32 = jnp.float32
bf16 = jnp.bfloat16

NZ, NYH, NC, NYL, NX = 8, 4, 2, 2, 4
ROWS, CH, TAPS, LANES = 128, 768, 31, 128
TILES = CH // LANES
HALF = CH // 2
REACH = 16
BLOCK = CH // (NZ * NYH * NC)
CHUNKS = HALF // LANES
NEAR = (0, 1, 7, 2, 6, 3, 5, 4)


def rem(a, b):
    return lax.rem(a, jnp.int32(b))


def div(a, b):
    return lax.div(a, jnp.int32(b))


def lanes_of(c, first=0):
    return pl.ds(pl.multiple_of(first + c * LANES, LANES), LANES)


def tiles(fn):
    def step(c, carry):
        fn(c)
        return carry

    lax.fori_loop(0, TILES, step, 0)


def fused(glu_hbm, len_ref, kern_hbm, gain_in, bias_in, w_hbm, cot_hbm,
          out_hbm, gg_hbm, gp_ref, gk_ref, gn_ref, gb_ref,
          glu, cot, kern, unit, conv, fac, dwide, da, act, out, gg, ub,
          wl, wr, wb, wfull, hs, hr, ds_, dr_, a1, a2, a3, b1, b2, b3, stat,
          kt, kr, k2, k3, kf, uq, ur, u2, gown, gsend, grc, gxs, gxr, gyf, gys, gyr, gz, gzs, gzr, fin, fb,
          hz, hzr, hy, hyr, hx, hfin, hfb,
          gain_v, bias_v, ssem, rsem, lsem):
    dp = lax.axis_index("dp")
    ctx = lax.axis_index("ctx")
    z, yh, core = div(dp, 8), rem(div(dp, 2), 4), rem(dp, 2)
    yl, x = div(ctx, 4), rem(ctx, 4)
    y = yh * 2 + yl
    g = x * 2 + core
    sib = 1 - core

    def dev(z_, y_, x_, c_):
        return (z_ * 8 + div(y_, 2) * 2 + c_, rem(y_, 2) * 4 + x_)

    def on_g(j):
        return dev(z, y, div(j, 2), rem(j, 2))

    def on_y(j):
        return dev(z, j, x, core)

    def on_z(j):
        return dev(j, y, x, core)

    def on_x(j):
        return dev(z, y, j, core)

    sibling = dev(z, y, x, sib)
    used = [0, 0]
    pending = []
    cond = []

    def ssems(n=1):
        used[0] += n
        return used[0] - n

    def rsems(n=1):
        used[1] += n
        return used[1] - n

    def desc(src, dst, ssend, recv, target):
        return pltpu.make_async_remote_copy(
            src_ref=src, dst_ref=dst, send_sem=ssem.at[ssend], recv_sem=rsem.at[recv],
            device_id=target, device_id_type=pl.DeviceIdType.MESH)

    def copy(src, dst, recv, target):
        return desc(src, dst, ssems(), recv, target)

    def send(src, dst, recv, target):
        c = copy(src, dst, recv, target)
        c.start()
        pending.append(c)

    def group(copies, total, recv):
        sem = ssems()
        for src, dst, target in copies:
            desc(src, dst, sem, recv, target).start()
        pending.append(desc(total, total, sem, recv, sibling))

    def arrived(dst, recv):
        desc(dst, dst, 0, recv, sibling).wait_recv()

    def finish():
        for c in pending:
            c.wait_send()
        for when, copies in cond:
            @pl.when(when)
            def _():
                for c in copies:
                    c.wait_send()

    def exchange(buf, me, where, n=8):
        recv = rsems()
        others = buf.at[pl.ds(0, n - 1)]
        group([(buf.at[me], buf.at[me], where(rem(me + d, n))) for d in range(1, n)], others, recv)
        return lambda: arrived(others, recv)

    def scatter(src_of, dst_of, total_src, total_dst, me, where, n=8):
        recv = rsems()
        copies = []
        for d in range(1, n):
            j = rem(me + d, n)
            copies.append((src_of(j), dst_of(d), where(j)))
        group(copies, total_src, recv)
        return lambda: arrived(total_dst, recv)

    barrier = pltpu.get_barrier_semaphore()
    peers = [on_g(rem(g + d, 8)) for d in range(1, 8)]
    peers += [on_y(rem(y + d, 8)) for d in range(1, 8)]
    peers += [on_z(rem(z + d, 8)) for d in range(1, 8)]
    flip = yh * 2 + (1 - yl)
    peers += [dev(z, rem(y + 2 * d, 8), x, sib) for d in range(1, 4)]
    peers += [dev(z, flip, div(rem(g + d, 8), 2), rem(rem(g + d, 8), 2)) for d in range(1, 8)]
    for p in peers:
        pl.semaphore_signal(barrier, inc=1, device_id=p, device_id_type=pl.DeviceIdType.MESH)

    loads = [pltpu.make_async_copy(a, b, lsem.at[i]) for i, (a, b) in enumerate(
        [(glu_hbm, glu), (kern_hbm, kern), (cot_hbm, cot), (gain_in, gain_v), (bias_in, bias_v)])]
    load_w = pltpu.make_async_copy(w_hbm, wl, lsem.at[5])

    @pl.when(yh == x)
    def _():
        load_w.start()

    for c in loads:
        c.start()

    pos0 = ctx * ROWS
    length = len_ref[0]
    n_live = jnp.clip(length - pos0, 0, ROWS).astype(f32)

    def live():
        return (lax.broadcasted_iota(jnp.int32, (ROWS, LANES), 0) + pos0 < length).astype(f32)

    pl.semaphore_wait(barrier, len(peers))

    own_cols = pl.ds(pl.multiple_of(core * HALF, LANES), HALF)
    sib_cols = pl.ds(pl.multiple_of(sib * HALF, LANES), HALF)
    w1, w2, w3, w4 = rsems(2), rsems(2), rsems(8), rsems(2)
    mine = wb.at[core, x, 0]
    groups = ((0, 5), (5, 3))
    w4_sems = []
    w1_sends = [copy(wl.at[:, sib_cols], wr.at[core], w1 + core, sibling)]
    for d in range(1, 4):
        y_ = rem(yh + d, 4) * 2 + yl
        w1_sends.append(copy(wl.at[:, own_cols], wr.at[core], w1 + core, dev(z, y_, x, core)))
        w1_sends.append(copy(wl.at[:, sib_cols], wr.at[core], w1 + core, dev(z, y_, x, sib)))
    cond.append((yh == x, w1_sends))

    @pl.when(yh == x)
    def _():
        load_w.wait()
        for c in w1_sends:
            c.start()
        wr[core] = wl[:, own_cols]

    def w1_done():
        @pl.when(yh != x)
        def _():
            arrived(wr.at[core], w1 + core)

        arrived(wr.at[sib], w1 + sib)
        rows = jnp.concatenate([wr[0].astype(f32), wr[1].astype(f32)], 0)
        wb[core, x, 0] = rows.reshape(3, 8, HALF).astype(bf16)
        for i, (first, size) in enumerate(groups):
            places = range(max(first, 1), first + size)
            group([(mine, wb.at[core, x, p], on_z(rem(z + 8 - NEAR[p], 8))) for p in places],
                  wb.at[core, x, pl.ds(places[0], len(places))], w2 + i)

    loads[0].wait()

    @tiles
    def _(c):
        v = glu[:, lanes_of(c)].astype(f32)
        sg = jax.nn.sigmoid(glu[:, lanes_of(c, CH)].astype(f32))
        u = (live() * v * sg).astype(bf16)
        hs[0, :, lanes_of(c)] = u[:REACH]
        hs[1, :, lanes_of(c)] = u[ROWS - REACH:]
        ub[pl.ds(REACH, ROWS), lanes_of(c)] = u
        unit[c, pl.ds(REACH, ROWS), :] = u.astype(f32)

    @pl.when(ctx == 0)
    def _():
        hr[0] = jnp.zeros((REACH, CH), bf16)
        dr_[0] = jnp.zeros((REACH, CH), bf16)

    @pl.when(ctx == 7)
    def _():
        hr[1] = jnp.zeros((REACH, CH), bf16)
        dr_[1] = jnp.zeros((REACH, CH), bf16)


    def halo(src, dst):
        base = rsems(2)
        to_left = copy(src.at[0], dst.at[1], base + 1, (dp, ctx - 1))
        to_right = copy(src.at[1], dst.at[0], base, (dp, ctx + 1))

        @pl.when(ctx > 0)
        def _():
            to_left.start()

        @pl.when(ctx < 7)
        def _():
            to_right.start()

        def done():
            @pl.when(ctx > 0)
            def _():
                arrived(dst.at[0], base)
                to_left.wait_send()

            @pl.when(ctx < 7)
            def _():
                arrived(dst.at[1], base + 1)
                to_right.wait_send()

        return done

    halo_done = halo(hs, hr)

    halo_done()
    for c in (loads[1], loads[3], loads[4]):
        c.wait()
    stat[6:7] = gain_v[...].reshape(1, CH)
    stat[7:8] = bias_v[...].reshape(1, CH)
    ub[pl.ds(0, REACH), :] = hr[0]
    ub[pl.ds(REACH + ROWS, REACH), :] = hr[1]

    @tiles
    def _(c):
        unit[c, pl.ds(0, REACH), :] = hr[0, :, lanes_of(c)].astype(f32)
        unit[c, pl.ds(REACH + ROWS, REACH), :] = hr[1, :, lanes_of(c)].astype(f32)
        acc = jnp.zeros((ROWS, LANES), f32)
        for k in range(TAPS):
            acc = acc + kern[pl.ds(k, 1), lanes_of(c)] * unit[c, pl.ds(k + 1, ROWS), :]
        conv[c] = acc
        m = live()
        s = jnp.sum(m * acc, 0, keepdims=True)
        centred = acc - s / jnp.maximum(n_live, 1.0)
        q = jnp.sum(m * centred * centred, 0, keepdims=True)
        a1[g, :, lanes_of(c)] = jnp.concatenate([s, q], 0)

    a1[g, :, pl.ds(CH, LANES)] = jnp.full((2, LANES), n_live, f32)

    def merged(buf):
        total = buf[0]
        for i in range(1, 8):
            total = total + buf[i]
        s, q, n = total[0:1, 0:CH], total[1:2, 0:CH], total[0:1, CH:]
        mean = s / jnp.maximum(jnp.concatenate([n] * TILES, 1), 1.0)
        for i in range(8):
            n_i = buf[i, 0:1, CH:]
            r_i = 1.0 / jnp.maximum(n_i, 1.0)
            off = buf[i, 0:1, 0:CH] - jnp.concatenate([n_i] * TILES, 1) * mean
            q = q + off * off * jnp.concatenate([r_i] * TILES, 1)
        return s, q, n

    def packed(s, q, n):
        return jnp.concatenate([jnp.concatenate([s, n], 1), jnp.concatenate([q, n], 1)], 0)

    def summed(buf):
        total = buf[0]
        for i in range(1, 8):
            total = total + buf[i]
        return total

    a_done = exchange(a1, g, on_g)

    w1_done()

    n_rows = jnp.clip(length - pos0, 0, ROWS)
    tap = lax.broadcasted_iota(jnp.int32, (32, ROWS + 2 * REACH), 0)
    row = lax.broadcasted_iota(jnp.int32, (32, ROWS + 2 * REACH), 1) - tap - 1
    window = ((row >= 0) & (row < n_rows) & (tap < TAPS)).astype(f32).astype(bf16)
    u_sum = jnp.dot(window, ub[...], preferred_element_type=f32)
    for j in range(8):
        uq[j, 0:4, :] = u_sum[4 * j:4 * j + 4]

    @tiles
    def _(c):
        at = lanes_of(c)
        d = live() * conv[c]
        for k in range(TAPS):
            uq[k // 4, pl.ds(4 + k % 4, 1), at] = jnp.sum(d * unit[c, pl.ds(k + 1, ROWS), :], 0, keepdims=True)
        uq[7, 7:8, at] = jnp.zeros((1, LANES), f32)

    a_done()
    a2[y] = packed(*merged(a1))
    a_done = exchange(a2, y, on_y)

    def onward(i):
        first, size = groups[i]
        some = max(first, 1)
        arrived(wb.at[core, x, pl.ds(some, first + size - some)], w2 + i)
        strip = wb.at[core, x, pl.ds(first, size)]
        sem = ssems()
        for d in range(1, 4):
            desc(strip, strip, sem, w3 + 4 * i + d, on_x(rem(x + d, 4))).start()
        pending.append(desc(wb.at[core, pl.ds(0, 3), pl.ds(first, size)],
                            wb.at[core, pl.ds(0, 3), pl.ds(first, size)], sem, 0, sibling))
        w4_sems.append(ssems())
        desc(strip, strip, w4_sems[i], w4 + i, sibling).start()

    def across(i):
        first, size = groups[i]
        for d in range(1, 4):
            piece = wb.at[core, rem(x + (4 - d), 4), pl.ds(first, size)]
            arrived(piece, w3 + 4 * i + d)
            desc(piece, piece, w4_sems[i], w4 + i, sibling).start()
        whole = wb.at[core, :, pl.ds(first, size)]
        pending.append(desc(whole, whole, w4_sems[i], 0, sibling))

    onward(0)
    onward(1)
    a_done()
    a3[z] = packed(*merged(a2))
    a_done = exchange(a3, z, on_z)
    uq_done = scatter(lambda j: uq.at[j], lambda d: ur.at[d], uq.at[pl.ds(0, 7)], ur.at[pl.ds(1, 7)], g, on_g)
    across(0)
    a_done()
    s, q, n = merged(a3)
    n = jnp.concatenate([n] * TILES, 1)
    stat[0:1] = s / n
    stat[1:2] = lax.rsqrt(q / n + eps)
    stat[2:3] = 1.0 / n
    stat[3:4] = lax.rsqrt(n)

    @tiles
    def _(c):
        at = lanes_of(c)
        normed = (conv[c] - stat[0:1, at]) * stat[1:2, at]
        conv[c] = normed
        pre = stat[6:7, at] * normed + stat[7:8, at]
        sp = jax.nn.sigmoid(pre)
        m = live()
        act[:, at] = (m * pre * sp).astype(bf16)
        fac[c] = m * sp * (1.0 + pre * (1.0 - sp))

    across(1)
    for i, (first, size) in enumerate(groups):
        arrived(wb.at[sib, :, pl.ds(first, size)], w4 + i)
    for p in range(NZ):
        rows = pl.ds(pl.multiple_of(rem(z + NEAR[p], 8) * 96, 16), 96)
        for h in range(2):
            wfull[h, rows, :] = wb[h, :, p].astype(f32).reshape(96, HALF).astype(bf16)
    uq_done()
    t = uq[g]
    for d in range(1, 8):
        t = t + ur[d]
    u2[y] = t
    u_done = exchange(u2, y, on_y)
    loads[2].wait()
    nt = (((1,), (1,)), ((), ()))
    da[...] = (lax.dot_general(cot[:, 0:HALF], wfull[0], nt, preferred_element_type=f32)
               + lax.dot_general(cot[:, HALF:CH], wfull[1], nt, preferred_element_type=f32))

    @tiles
    def _(c):
        at = lanes_of(c)
        d_pre = da[:, at] * fac[c]
        fac[c] = d_pre
        b1[g, :, at] = jnp.concatenate(
            [jnp.sum(d_pre, 0, keepdims=True), jnp.sum(d_pre * conv[c], 0, keepdims=True)], 0)

    b_done = exchange(b1, g, on_g)

    tn = (((0,), (0,)), ((), ()))

    gc, h3 = rsems(CHUNKS), rsems(CHUNKS)
    h1_done, h2_done = {}, {}

    @tiles
    def _(c):
        at = lanes_of(c)
        rows = pl.ds(pl.multiple_of(c * LANES, LANES), LANES)
        a = act[:, at]
        g_sib = lax.dot_general(a, cot[:, sib_cols], tn, preferred_element_type=f32).astype(bf16)
        g_own = lax.dot_general(a, cot[:, own_cols], tn, preferred_element_type=f32)
        for q in range(CHUNKS):
            gsend[q, rows, :] = g_sib[:, q * LANES:(q + 1) * LANES]
            gown[q, rows, :] = g_own[:, q * LANES:(q + 1) * LANES]
        d = fac[c]
        for k in range(TAPS):
            kt[k // 4, pl.ds(k % 4, 1), at] = jnp.sum(d * unit[c, pl.ds(k + 1, ROWS), :], 0, keepdims=True)
        kt[7, 3:4, at] = jnp.zeros((1, LANES), f32)

    for q in range(CHUNKS):
        send(gsend.at[q], grc.at[q], gc + q, sibling)
    k1_done = scatter(lambda j: kt.at[j], lambda d: kr.at[d], kt.at[pl.ds(0, 7)], kr.at[pl.ds(1, 7)], g, on_g)
    gx_done = []

    def x_send(q):
        return scatter(lambda j: gxs.at[q, j], lambda d: gxr.at[q, d],
                       gxs.at[q, pl.ds(0, 3)], gxr.at[q, pl.ds(1, 3)], x, on_x, NX)

    for q in (0, 1):
        arrived(grc.at[q], gc + q)
        t = gown[q] + grc[q].astype(f32)
        gown[q] = t
        gxs[q] = t.astype(bf16).reshape(NX, 192, LANES)
        gx_done.append(x_send(q))

    b_done()
    b2[z] = summed(b1)
    b_done = exchange(b2, z, on_z)

    arrived(grc.at[2], gc + 2)
    t = gown[2] + grc[2].astype(f32)
    gown[2] = t
    hz[2] = t.astype(bf16).reshape(NZ, 96, LANES)
    h1_done[2] = scatter(lambda j: hz.at[2, j], lambda d: hzr.at[2, d],
                         hz.at[2, pl.ds(0, 7)], hzr.at[2, pl.ds(1, 7)], z, on_z)

    k1_done()
    t = kt[g]
    for d in range(1, 8):
        t = t + kr[d]
    k2[y] = t
    k_done = exchange(k2, y, on_y)
    b_done()
    b3[y] = summed(b2)
    b_done = exchange(b3, y, on_y)

    def x_part(q):
        gx_done[q]()
        t = gown[q, pl.ds(pl.multiple_of(x * 192, 16), 192), :]
        for d in range(1, 4):
            t = t + gxr[q, d].astype(f32)
        t = t.reshape(24, 8, LANES)
        gyf[q] = t
        gys[q] = t.astype(bf16)
        return scatter(lambda j: gys.at[q, pl.ds(rem(j, 2) * 12 + div(j, 2) * 3, 3)], lambda d: gyr.at[q, d],
                       gyr.at[q, pl.ds(0, 7)], gyr.at[q, pl.ds(1, 7)], y, on_y)

    def z_part(q):
        h1_done[q]()
        t = gown[q, pl.ds(pl.multiple_of(z * 96, 16), 96), :]
        for d in range(1, 8):
            t = t + hzr[q, d].astype(f32)
        hy[q] = t.reshape(12, 8, LANES).astype(bf16)
        h2_done[q] = scatter(lambda j: hy.at[q, pl.ds(div(j, 2) * 3, 3)], lambda d: hyr.at[q, y],
                             hyr.at[q, pl.ds(0, 7)], hyr.at[q, pl.ds(0, 7)], y, on_y)
        hyr[q, y] = hy[q, pl.ds(yh * 3, 3)]

    def zy_part(q):
        h2_done[q]()
        t = hyr[q, 0].astype(f32)
        for i in range(1, 8):
            t = t + hyr[q, i].astype(f32)
        hx[q, x] = t
        return exchange(hx.at[q], x, on_x, NX)

    def zyx_part(q, done):
        done()
        t = hx[q, 0]
        for i in range(1, NX):
            t = t + hx[q, i]
        hfin[q] = t * stat[3:4, 0:LANES].reshape(1, 1, LANES)
        send(hfin.at[q, pl.ds(sib, 2)], hfb.at[core, q], h3 + q, sibling)
        hfb[core, q] = hfin[q, pl.ds(core, 2)]

    gy_done = [x_part(0), x_part(1)]
    for h in range(2):
        out[:, h * HALF:(h + 1) * HALF] = jnp.dot(act[...], wfull[h], preferred_element_type=f32).astype(bf16)
    store_out = pltpu.make_async_copy(out, out_hbm, lsem.at[6])
    store_out.start()
    b_done()
    sums = summed(b3)
    gb_ref[...] = (sums[0:1] * stat[3:4]).reshape(CH)
    gn_ref[...] = (sums[1:2] * stat[3:4]).reshape(CH)
    stat[4:5] = sums[0:1] * stat[2:3]
    stat[5:6] = sums[1:2] * stat[2:3]

    @tiles
    def _(c):
        at = lanes_of(c)
        d = (live() * (stat[6:7, at] * stat[1:2, at])
             * (fac[c] - stat[4:5, at] - conv[c] * stat[5:6, at])).astype(bf16)
        ds_[0, :, at] = d[:REACH]
        ds_[1, :, at] = d[ROWS - REACH:]
        dwide[c, pl.ds(REACH, ROWS), :] = d.astype(f32)

    halo_done = halo(ds_, dr_)

    u_done()
    u_all = summed(u2)
    k_done()
    u_rows, q_rows = u_all[0:4], u_all[4:8]
    inv = stat[1:2]
    k3[z] = (stat[6:7] * inv) * (
        summed(k2) - stat[4:5] * u_rows - stat[5:6] * (inv * (q_rows - stat[0:1] * u_rows)))
    k_done = exchange(k3, z, on_z)

    owner = 2 * x + yl
    gzb = rsems()
    slot = rem(z + 8 - owner, 8)

    def y_part(q):
        gy_done[q]()
        t = gyf[q, pl.ds(yl * 12 + yh * 3, 3)]
        for d in range(1, 8):
            t = t + gyr[q, d].astype(f32)
        gz[q] = t
        gzs[q] = t.astype(bf16)

    z_part(2)
    y_part(0)
    y_part(1)
    to_owner = copy(gzs, gzr.at[slot], gzb, on_z(owner))
    cond.append((z != owner, [to_owner]))

    @pl.when(z != owner)
    def _():
        to_owner.start()

    halo_done()

    @tiles
    def _(c):
        at = lanes_of(c)
        dwide[c, pl.ds(0, REACH), :] = dr_[0, :, at].astype(f32)
        dwide[c, pl.ds(REACH + ROWS, REACH), :] = dr_[1, :, at].astype(f32)
        acc = jnp.zeros((ROWS, LANES), f32)
        for k in range(TAPS):
            acc = acc + kern[pl.ds(k, 1), at] * dwide[c, pl.ds(TAPS - k, ROWS), :]
        v = glu[:, at].astype(f32)
        sg = jax.nn.sigmoid(glu[:, lanes_of(c, CH)].astype(f32))
        du = live() * acc * sg
        gg[:, at] = du.astype(bf16)
        gg[:, lanes_of(c, CH)] = (du * v * (1.0 - sg)).astype(bf16)

    store_gg = pltpu.make_async_copy(gg, gg_hbm, lsem.at[7])
    store_gg.start()

    x2_done = zy_part(2)
    k_done()
    kf[g] = summed(k3) * stat[3:4]
    k_done = exchange(kf, g, on_g)

    fbb = rsems(2)
    spread = []
    for d in range(1, 16):
        e = rem(core + d, 2)
        c_ = rem(ctx + d // 2, 8)
        spread.append(copy(fin.at[pl.ds(e, 2)], fb.at[core], fbb + core, (div(dp, 2) * 2 + e, c_)))
    cond.append((z == owner, spread))

    @pl.when(z == owner)
    def _():
        arrived(gzr.at[pl.ds(1, 7)], gzb)
        for q in (0, 1):
            t = gz[q]
            for d in range(1, 8):
                t = t + gzr[d, q].astype(f32)
            t = t * stat[3:4, 0:LANES].reshape(1, 1, LANES)
            for u in range(3):
                fin[u, q] = t[u]
        for c in spread:
            c.start()
        fb[core] = fin[pl.ds(core, 2)]

    zyx_part(2, x2_done)
    k_done()
    for j in range(8):
        w = 4 if j < 7 else 3
        gk_ref[pl.ds(4 * j, w), :] = kf[j, 0:w, :]

    @pl.when(z != owner)
    def _():
        arrived(fb.at[core], fbb + core)

    arrived(fb.at[sib], fbb + sib)
    arrived(hfb.at[sib, 2], h3 + 2)
    for h in range(2):
        for q in range(CHUNKS):
            v = jnp.concatenate([fb[h, 0, q], fb[h, 1, q]], 0) if q < 2 else hfb[h, q].reshape(16, LANES)
            gp_ref[:, pl.ds(h * HALF + q * LANES, LANES)] = jnp.where(core == 0, v[0:BLOCK], v[16 - BLOCK:16])

    finish()
    store_out.wait()
    store_gg.wait()


def handed_on(*refs):
    sem = refs[12]
    copies = [pltpu.make_async_copy(refs[i], refs[6 + i], sem.at[i]) for i in range(6)]
    for c in copies:
        c.start()
    for c in copies:
        c.wait()


def body(glu_in, lengths, kernel, bn_gain, bn_bias, proj_weight, cotangent):
    vm = pltpu.VMEM
    hbm = functools.partial(pltpu.with_memory_space_constraint, memory_space=pltpu.HBM)
    anyspec = pl.BlockSpec(memory_space=pl.ANY)
    vspec = pl.BlockSpec(memory_space=pltpu.VMEM)
    sspec = pl.BlockSpec(memory_space=pltpu.SMEM)
    scratch = [
        vm((ROWS, 2 * CH), bf16), vm((ROWS, CH), bf16), vm((TAPS, CH), f32),
        vm((TILES, ROWS + 2 * REACH, LANES), f32), vm((TILES, ROWS, LANES), f32),
        vm((TILES, ROWS, LANES), f32), vm((TILES, ROWS + 2 * REACH, LANES), f32),
        vm((ROWS, CH), f32), vm((ROWS, CH), bf16), vm((ROWS, CH), bf16), vm((ROWS, 2 * CH), bf16),
        vm((ROWS + 2 * REACH, CH), bf16),
        vm((BLOCK, CH), bf16), vm((NC, BLOCK, HALF), bf16),
        vm((NC, NYH, NZ, 3, 8, HALF), bf16), vm((NC, CH, HALF), bf16),
        vm((2, REACH, CH), bf16), vm((2, REACH, CH), bf16), vm((2, REACH, CH), bf16), vm((2, REACH, CH), bf16),
        vm((8, 2, CH + LANES), f32), vm((8, 2, CH + LANES), f32), vm((8, 2, CH + LANES), f32),
        vm((8, 2, CH), f32), vm((8, 2, CH), f32), vm((8, 2, CH), f32),
        vm((8, CH), f32),
        vm((8, 4, CH), f32), vm((8, 4, CH), f32), vm((8, 4, CH), f32), vm((8, 4, CH), f32), vm((8, 4, CH), f32),
        vm((8, 8, CH), f32), vm((8, 8, CH), f32), vm((8, 8, CH), f32),
        vm((CHUNKS, CH, LANES), f32), vm((CHUNKS, CH, LANES), bf16), vm((CHUNKS, CH, LANES), bf16),
        vm((2, NX, 192, LANES), bf16), vm((2, NX, 192, LANES), bf16),
        vm((2, 24, 8, LANES), f32), vm((2, 24, 8, LANES), bf16), vm((2, 8, 3, 8, LANES), bf16),
        vm((2, 3, 8, LANES), f32), vm((2, 3, 8, LANES), bf16), vm((8, 2, 3, 8, LANES), bf16),
        vm((3, 2, 8, LANES), f32), vm((2, 2, 2, 8, LANES), f32),
        vm((CHUNKS, NZ, 96, LANES), bf16), vm((CHUNKS, NZ, 96, LANES), bf16),
        vm((CHUNKS, 12, 8, LANES), bf16), vm((CHUNKS, 8, 3, 8, LANES), bf16),
        vm((CHUNKS, NX, 3, 8, LANES), f32), vm((CHUNKS, 3, 8, LANES), f32), vm((2, CHUNKS, 2, 8, LANES), f32),
        vm((CH,), f32), vm((CH,), f32),
        pltpu.SemaphoreType.DMA((64,)), pltpu.SemaphoreType.DMA((64,)), pltpu.SemaphoreType.DMA((8,)),
    ]
    outs = [
        jax.ShapeDtypeStruct((ROWS, CH), bf16),
        jax.ShapeDtypeStruct((ROWS, 2 * CH), bf16),
        jax.ShapeDtypeStruct((BLOCK, CH), f32),
        jax.ShapeDtypeStruct((TAPS, CH), f32),
        jax.ShapeDtypeStruct((CH,), f32),
        jax.ShapeDtypeStruct((CH,), f32),
    ]
    results = pl.pallas_call(
        fused,
        out_shape=outs,
        in_specs=[anyspec, sspec, anyspec, anyspec, anyspec, anyspec, anyspec],
        out_specs=[anyspec, anyspec, vspec, vspec, vspec, vspec],
        scratch_shapes=scratch,
        compiler_params=pltpu.CompilerParams(
            collective_id=0, has_side_effects=True, vmem_limit_bytes=40 * 1024 * 1024),
        name="conformer_conv",
    )(hbm(glu_in[0]), lengths, hbm(kernel), hbm(bn_gain), hbm(bn_bias), hbm(proj_weight), hbm(cotangent[0]))
    result, grad_glu, grad_proj, grad_kernel, grad_gain, grad_bias = pl.pallas_call(
        handed_on,
        out_shape=outs,
        in_specs=[anyspec] * 6,
        out_specs=[anyspec] * 6,
        scratch_shapes=[pltpu.SemaphoreType.DMA((6,))],
        compiler_params=pltpu.CompilerParams(vmem_limit_bytes=1024 * 1024),
        name="handed_on",
    )(*results)
    return (result[None], grad_glu[None], grad_proj, grad_kernel, grad_gain, grad_bias)


def solution(mesh):
    in_specs = (P("dp", "ctx", None), P("dp"), P(), P(), P(), P("dp", None), P("dp", "ctx", None))
    out_specs = (P("dp", "ctx", None), P("dp", "ctx", None), P("dp", None), P(), P(), P())
    return jax.shard_map(body, mesh=mesh, in_specs=in_specs, out_specs=out_specs, check_vma=False)
```

```python
import functools

import jax
import jax.numpy as jnp
from jax import lax
from jax.experimental import pallas as pl
from jax.experimental.pallas import tpu as pltpu
from jax.sharding import PartitionSpec as P

eps = 1e-05
f32 = jnp.float32
bf16 = jnp.bfloat16

NZ, NYH, NC, NYL, NX = 8, 4, 2, 2, 4
ROWS, CH, TAPS, LANES = 128, 768, 31, 128
TILES = CH // LANES
HALF = CH // 2
REACH = 16
BLOCK = CH // (NZ * NYH * NC)
CHUNKS = HALF // LANES
NEAR = (0, 1, 7, 2, 6, 3, 5, 4)


def rem(a, b):
    return lax.rem(a, jnp.int32(b))


def div(a, b):
    return lax.div(a, jnp.int32(b))


def lanes_of(c, first=0):
    return pl.ds(pl.multiple_of(first + c * LANES, LANES), LANES)


def tiles(fn):
    def step(c, carry):
        fn(c)
        return carry

    lax.fori_loop(0, TILES, step, 0)


def fused(glu_hbm, len_ref, kern_hbm, gain_in, bias_in, w_hbm, cot_hbm,
          out_hbm, gg_hbm, gp_ref, gk_ref, gn_ref, gb_ref,
          glu, cot, kern, unit, conv, fac, dwide, da, act, out, gg, ub,
          wl, wr, wb, wfull, hs, hr, ds_, dr_, a1, a2, a3, b1, b2, b3, stat,
          kt, kr, k2, k3, kf, uq, ur, u2, gown, gsend, grc, gxs, gxr, gyf, gys, gyr, gz, gzs, gzr, fin, fb,
          hz, hzr, hy, hyr, hx, hfin, hfb,
          gain_v, bias_v, ssem, rsem, lsem):
    dp = lax.axis_index("dp")
    ctx = lax.axis_index("ctx")
    z, yh, core = div(dp, 8), rem(div(dp, 2), 4), rem(dp, 2)
    yl, x = div(ctx, 4), rem(ctx, 4)
    y = yh * 2 + yl
    g = x * 2 + core
    sib = 1 - core

    def dev(z_, y_, x_, c_):
        return (z_ * 8 + div(y_, 2) * 2 + c_, rem(y_, 2) * 4 + x_)

    def on_g(j):
        return dev(z, y, div(j, 2), rem(j, 2))

    def on_y(j):
        return dev(z, j, x, core)

    def on_z(j):
        return dev(j, y, x, core)

    def on_x(j):
        return dev(z, y, j, core)

    sibling = dev(z, y, x, sib)
    used = [0, 0]
    pending = []
    cond = []

    def ssems(n=1):
        used[0] += n
        return used[0] - n

    def rsems(n=1):
        used[1] += n
        return used[1] - n

    def desc(src, dst, ssend, recv, target):
        return pltpu.make_async_remote_copy(
            src_ref=src, dst_ref=dst, send_sem=ssem.at[ssend], recv_sem=rsem.at[recv],
            device_id=target, device_id_type=pl.DeviceIdType.MESH)

    def copy(src, dst, recv, target):
        return desc(src, dst, ssems(), recv, target)

    def send(src, dst, recv, target):
        c = copy(src, dst, recv, target)
        c.start()
        pending.append(c)

    def group(copies, total, recv):
        sem = ssems()
        for src, dst, target in copies:
            desc(src, dst, sem, recv, target).start()
        pending.append(desc(total, total, sem, recv, sibling))

    def arrived(dst, recv):
        desc(dst, dst, 0, recv, sibling).wait_recv()

    def finish():
        for c in pending:
            c.wait_send()
        for when, copies in cond:
            @pl.when(when)
            def _():
                for c in copies:
                    c.wait_send()

    def exchange(buf, me, where, n=8):
        recv = rsems()
        others = buf.at[pl.ds(0, n - 1)]
        group([(buf.at[me], buf.at[me], where(rem(me + d, n))) for d in range(1, n)], others, recv)
        return lambda: arrived(others, recv)

    def scatter(src_of, dst_of, total_src, total_dst, me, where, n=8):
        recv = rsems()
        copies = []
        for d in range(1, n):
            j = rem(me + d, n)
            copies.append((src_of(j), dst_of(d), where(j)))
        group(copies, total_src, recv)
        return lambda: arrived(total_dst, recv)

    barrier = pltpu.get_barrier_semaphore()
    peers = [on_g(rem(g + d, 8)) for d in range(1, 8)]
    peers += [on_y(rem(y + d, 8)) for d in range(1, 8)]
    peers += [on_z(rem(z + d, 8)) for d in range(1, 8)]
    flip = yh * 2 + (1 - yl)
    peers += [dev(z, rem(y + 2 * d, 8), x, sib) for d in range(1, 4)]
    peers += [dev(z, flip, div(rem(g + d, 8), 2), rem(rem(g + d, 8), 2)) for d in range(1, 8)]
    for p in peers:
        pl.semaphore_signal(barrier, inc=1, device_id=p, device_id_type=pl.DeviceIdType.MESH)

    loads = [pltpu.make_async_copy(a, b, lsem.at[i]) for i, (a, b) in enumerate(
        [(glu_hbm, glu), (kern_hbm, kern), (cot_hbm, cot), (gain_in, gain_v), (bias_in, bias_v)])]
    load_w = pltpu.make_async_copy(w_hbm, wl, lsem.at[5])

    @pl.when(yh == x)
    def _():
        load_w.start()

    for c in loads:
        c.start()

    pos0 = ctx * ROWS
    length = len_ref[0]
    n_live = jnp.clip(length - pos0, 0, ROWS).astype(f32)

    def live():
        return (lax.broadcasted_iota(jnp.int32, (ROWS, LANES), 0) + pos0 < length).astype(f32)

    pl.semaphore_wait(barrier, len(peers))

    own_cols = pl.ds(pl.multiple_of(core * HALF, LANES), HALF)
    sib_cols = pl.ds(pl.multiple_of(sib * HALF, LANES), HALF)
    w1, w2, w3, w4 = rsems(2), rsems(2), rsems(8), rsems(2)
    mine = wb.at[core, x, 0]
    groups = ((0, 5), (5, 3))
    w4_sems = []
    w1_sends = [copy(wl.at[:, sib_cols], wr.at[core], w1 + core, sibling)]
    for d in range(1, 4):
        y_ = rem(yh + d, 4) * 2 + yl
        w1_sends.append(copy(wl.at[:, own_cols], wr.at[core], w1 + core, dev(z, y_, x, core)))
        w1_sends.append(copy(wl.at[:, sib_cols], wr.at[core], w1 + core, dev(z, y_, x, sib)))
    cond.append((yh == x, w1_sends))

    @pl.when(yh == x)
    def _():
        load_w.wait()
        for c in w1_sends:
            c.start()
        wr[core] = wl[:, own_cols]

    def w1_done():
        @pl.when(yh != x)
        def _():
            arrived(wr.at[core], w1 + core)

        arrived(wr.at[sib], w1 + sib)
        rows = jnp.concatenate([wr[0].astype(f32), wr[1].astype(f32)], 0)
        wb[core, x, 0] = rows.reshape(3, 8, HALF).astype(bf16)
        for i, (first, size) in enumerate(groups):
            places = range(max(first, 1), first + size)
            group([(mine, wb.at[core, x, p], on_z(rem(z + 8 - NEAR[p], 8))) for p in places],
                  wb.at[core, x, pl.ds(places[0], len(places))], w2 + i)

    loads[0].wait()

    @tiles
    def _(c):
        v = glu[:, lanes_of(c)].astype(f32)
        sg = jax.nn.sigmoid(glu[:, lanes_of(c, CH)].astype(f32))
        u = (live() * v * sg).astype(bf16)
        hs[0, :, lanes_of(c)] = u[:REACH]
        hs[1, :, lanes_of(c)] = u[ROWS - REACH:]
        ub[pl.ds(REACH, ROWS), lanes_of(c)] = u
        unit[c, pl.ds(REACH, ROWS), :] = u.astype(f32)

    @pl.when(ctx == 0)
    def _():
        hr[0] = jnp.zeros((REACH, CH), bf16)
        dr_[0] = jnp.zeros((REACH, CH), bf16)

    @pl.when(ctx == 7)
    def _():
        hr[1] = jnp.zeros((REACH, CH), bf16)
        dr_[1] = jnp.zeros((REACH, CH), bf16)


    def halo(src, dst):
        base = rsems(2)
        to_left = copy(src.at[0], dst.at[1], base + 1, (dp, ctx - 1))
        to_right = copy(src.at[1], dst.at[0], base, (dp, ctx + 1))

        @pl.when(ctx > 0)
        def _():
            to_left.start()

        @pl.when(ctx < 7)
        def _():
            to_right.start()

        def done():
            @pl.when(ctx > 0)
            def _():
                arrived(dst.at[0], base)
                to_left.wait_send()

            @pl.when(ctx < 7)
            def _():
                arrived(dst.at[1], base + 1)
                to_right.wait_send()

        return done

    halo_done = halo(hs, hr)

    halo_done()
    for c in (loads[1], loads[3], loads[4]):
        c.wait()
    stat[6:7] = gain_v[...].reshape(1, CH)
    stat[7:8] = bias_v[...].reshape(1, CH)
    ub[pl.ds(0, REACH), :] = hr[0]
    ub[pl.ds(REACH + ROWS, REACH), :] = hr[1]

    @tiles
    def _(c):
        unit[c, pl.ds(0, REACH), :] = hr[0, :, lanes_of(c)].astype(f32)
        unit[c, pl.ds(REACH + ROWS, REACH), :] = hr[1, :, lanes_of(c)].astype(f32)
        acc = jnp.zeros((ROWS, LANES), f32)
        for k in range(TAPS):
            acc = acc + kern[pl.ds(k, 1), lanes_of(c)] * unit[c, pl.ds(k + 1, ROWS), :]
        conv[c] = acc
        m = live()
        s = jnp.sum(m * acc, 0, keepdims=True)
        centred = acc - s / jnp.maximum(n_live, 1.0)
        q = jnp.sum(m * centred * centred, 0, keepdims=True)
        a1[g, :, lanes_of(c)] = jnp.concatenate([s, q], 0)

    a1[g, :, pl.ds(CH, LANES)] = jnp.full((2, LANES), n_live, f32)

    def merged(buf):
        total = buf[0]
        for i in range(1, 8):
            total = total + buf[i]
        s, q, n = total[0:1, 0:CH], total[1:2, 0:CH], total[0:1, CH:]
        mean = s / jnp.maximum(jnp.concatenate([n] * TILES, 1), 1.0)
        for i in range(8):
            n_i = buf[i, 0:1, CH:]
            r_i = 1.0 / jnp.maximum(n_i, 1.0)
            off = buf[i, 0:1, 0:CH] - jnp.concatenate([n_i] * TILES, 1) * mean
            q = q + off * off * jnp.concatenate([r_i] * TILES, 1)
        return s, q, n

    def packed(s, q, n):
        return jnp.concatenate([jnp.concatenate([s, n], 1), jnp.concatenate([q, n], 1)], 0)

    def summed(buf):
        total = buf[0]
        for i in range(1, 8):
            total = total + buf[i]
        return total

    a_done = exchange(a1, g, on_g)

    w1_done()

    n_rows = jnp.clip(length - pos0, 0, ROWS)
    tap = lax.broadcasted_iota(jnp.int32, (32, ROWS + 2 * REACH), 0)
    row = lax.broadcasted_iota(jnp.int32, (32, ROWS + 2 * REACH), 1) - tap - 1
    window = ((row >= 0) & (row < n_rows) & (tap < TAPS)).astype(f32).astype(bf16)
    u_sum = jnp.dot(window, ub[...], preferred_element_type=f32)
    for j in range(8):
        uq[j, 0:4, :] = u_sum[4 * j:4 * j + 4]

    @tiles
    def _(c):
        at = lanes_of(c)
        d = live() * conv[c]
        for k in range(TAPS):
            uq[k // 4, pl.ds(4 + k % 4, 1), at] = jnp.sum(d * unit[c, pl.ds(k + 1, ROWS), :], 0, keepdims=True)
        uq[7, 7:8, at] = jnp.zeros((1, LANES), f32)

    a_done()
    a2[y] = packed(*merged(a1))
    a_done = exchange(a2, y, on_y)

    def onward(i):
        first, size = groups[i]
        some = max(first, 1)
        arrived(wb.at[core, x, pl.ds(some, first + size - some)], w2 + i)
        strip = wb.at[core, x, pl.ds(first, size)]
        sem = ssems()
        for d in range(1, 4):
            desc(strip, strip, sem, w3 + 4 * i + d, on_x(rem(x + d, 4))).start()
        pending.append(desc(wb.at[core, pl.ds(0, 3), pl.ds(first, size)],
                            wb.at[core, pl.ds(0, 3), pl.ds(first, size)], sem, 0, sibling))
        w4_sems.append(ssems())
        desc(strip, strip, w4_sems[i], w4 + i, sibling).start()

    def across(i):
        first, size = groups[i]
        for d in range(1, 4):
            piece = wb.at[core, rem(x + (4 - d), 4), pl.ds(first, size)]
            arrived(piece, w3 + 4 * i + d)
            desc(piece, piece, w4_sems[i], w4 + i, sibling).start()
        whole = wb.at[core, :, pl.ds(first, size)]
        pending.append(desc(whole, whole, w4_sems[i], 0, sibling))

    onward(0)
    onward(1)
    a_done()
    a3[z] = packed(*merged(a2))
    a_done = exchange(a3, z, on_z)
    uq_done = scatter(lambda j: uq.at[j], lambda d: ur.at[d], uq.at[pl.ds(0, 7)], ur.at[pl.ds(1, 7)], g, on_g)
    across(0)
    a_done()
    s, q, n = merged(a3)
    n = jnp.concatenate([n] * TILES, 1)
    stat[0:1] = s / n
    stat[1:2] = lax.rsqrt(q / n + eps)
    stat[2:3] = 1.0 / n
    stat[3:4] = lax.rsqrt(n)

    @tiles
    def _(c):
        at = lanes_of(c)
        normed = (conv[c] - stat[0:1, at]) * stat[1:2, at]
        conv[c] = normed
        pre = stat[6:7, at] * normed + stat[7:8, at]
        sp = jax.nn.sigmoid(pre)
        m = live()
        act[:, at] = (m * pre * sp).astype(bf16)
        fac[c] = m * sp * (1.0 + pre * (1.0 - sp))

    across(1)
    for i, (first, size) in enumerate(groups):
        arrived(wb.at[sib, :, pl.ds(first, size)], w4 + i)
    for p in range(NZ):
        rows = pl.ds(pl.multiple_of(rem(z + NEAR[p], 8) * 96, 16), 96)
        for h in range(2):
            wfull[h, rows, :] = wb[h, :, p].astype(f32).reshape(96, HALF).astype(bf16)
    uq_done()
    t = uq[g]
    for d in range(1, 8):
        t = t + ur[d]
    u2[y] = t
    u_done = exchange(u2, y, on_y)
    loads[2].wait()
    nt = (((1,), (1,)), ((), ()))
    da[...] = (lax.dot_general(cot[:, 0:HALF], wfull[0], nt, preferred_element_type=f32)
               + lax.dot_general(cot[:, HALF:CH], wfull[1], nt, preferred_element_type=f32))

    @tiles
    def _(c):
        at = lanes_of(c)
        d_pre = da[:, at] * fac[c]
        fac[c] = d_pre
        b1[g, :, at] = jnp.concatenate(
            [jnp.sum(d_pre, 0, keepdims=True), jnp.sum(d_pre * conv[c], 0, keepdims=True)], 0)

    b_done = exchange(b1, g, on_g)

    tn = (((0,), (0,)), ((), ()))

    gc, h3 = rsems(CHUNKS), rsems(CHUNKS)
    h1_done, h2_done = {}, {}

    @tiles
    def _(c):
        at = lanes_of(c)
        rows = pl.ds(pl.multiple_of(c * LANES, LANES), LANES)
        a = act[:, at]
        g_sib = lax.dot_general(a, cot[:, sib_cols], tn, preferred_element_type=f32).astype(bf16)
        g_own = lax.dot_general(a, cot[:, own_cols], tn, preferred_element_type=f32)
        for q in range(CHUNKS):
            gsend[q, rows, :] = g_sib[:, q * LANES:(q + 1) * LANES]
            gown[q, rows, :] = g_own[:, q * LANES:(q + 1) * LANES]
        d = fac[c]
        for k in range(TAPS):
            kt[k // 4, pl.ds(k % 4, 1), at] = jnp.sum(d * unit[c, pl.ds(k + 1, ROWS), :], 0, keepdims=True)
        kt[7, 3:4, at] = jnp.zeros((1, LANES), f32)

    for q in range(CHUNKS):
        send(gsend.at[q], grc.at[q], gc + q, sibling)
    k1_done = scatter(lambda j: kt.at[j], lambda d: kr.at[d], kt.at[pl.ds(0, 7)], kr.at[pl.ds(1, 7)], g, on_g)
    gx_done = []

    def x_send(q):
        return scatter(lambda j: gxs.at[q, j], lambda d: gxr.at[q, d],
                       gxs.at[q, pl.ds(0, 3)], gxr.at[q, pl.ds(1, 3)], x, on_x, NX)

    for q in (0, 1):
        arrived(grc.at[q], gc + q)
        t = gown[q] + grc[q].astype(f32)
        gown[q] = t
        gxs[q] = t.astype(bf16).reshape(NX, 192, LANES)
        gx_done.append(x_send(q))

    b_done()
    b2[z] = summed(b1)
    b_done = exchange(b2, z, on_z)

    arrived(grc.at[2], gc + 2)
    t = gown[2] + grc[2].astype(f32)
    gown[2] = t
    hz[2] = t.astype(bf16).reshape(NZ, 96, LANES)
    h1_done[2] = scatter(lambda j: hz.at[2, j], lambda d: hzr.at[2, d],
                         hz.at[2, pl.ds(0, 7)], hzr.at[2, pl.ds(1, 7)], z, on_z)

    k1_done()
    t = kt[g]
    for d in range(1, 8):
        t = t + kr[d]
    k2[y] = t
    k_done = exchange(k2, y, on_y)
    b_done()
    b3[y] = summed(b2)
    b_done = exchange(b3, y, on_y)

    def x_part(q):
        gx_done[q]()
        t = gown[q, pl.ds(pl.multiple_of(x * 192, 16), 192), :]
        for d in range(1, 4):
            t = t + gxr[q, d].astype(f32)
        t = t.reshape(24, 8, LANES)
        gyf[q] = t
        gys[q] = t.astype(bf16)
        return scatter(lambda j: gys.at[q, pl.ds(rem(j, 2) * 12 + div(j, 2) * 3, 3)], lambda d: gyr.at[q, d],
                       gyr.at[q, pl.ds(0, 7)], gyr.at[q, pl.ds(1, 7)], y, on_y)

    def z_part(q):
        h1_done[q]()
        t = gown[q, pl.ds(pl.multiple_of(z * 96, 16), 96), :]
        for d in range(1, 8):
            t = t + hzr[q, d].astype(f32)
        hy[q] = t.reshape(12, 8, LANES).astype(bf16)
        h2_done[q] = scatter(lambda j: hy.at[q, pl.ds(div(j, 2) * 3, 3)], lambda d: hyr.at[q, y],
                             hyr.at[q, pl.ds(0, 7)], hyr.at[q, pl.ds(0, 7)], y, on_y)
        hyr[q, y] = hy[q, pl.ds(yh * 3, 3)]

    def zy_part(q):
        h2_done[q]()
        t = hyr[q, 0].astype(f32)
        for i in range(1, 8):
            t = t + hyr[q, i].astype(f32)
        hx[q, x] = t
        return exchange(hx.at[q], x, on_x, NX)

    def zyx_part(q, done):
        done()
        t = hx[q, 0]
        for i in range(1, NX):
            t = t + hx[q, i]
        hfin[q] = t * stat[3:4, 0:LANES].reshape(1, 1, LANES)
        send(hfin.at[q, pl.ds(sib, 2)], hfb.at[core, q], h3 + q, sibling)
        hfb[core, q] = hfin[q, pl.ds(core, 2)]

    gy_done = [x_part(0), x_part(1)]
    for h in range(2):
        out[:, h * HALF:(h + 1) * HALF] = jnp.dot(act[...], wfull[h], preferred_element_type=f32).astype(bf16)
    store_out = pltpu.make_async_copy(out, out_hbm, lsem.at[6])
    store_out.start()
    z_part(2)
    b_done()
    sums = summed(b3)
    gb_ref[...] = (sums[0:1] * stat[3:4]).reshape(CH)
    gn_ref[...] = (sums[1:2] * stat[3:4]).reshape(CH)
    stat[4:5] = sums[0:1] * stat[2:3]
    stat[5:6] = sums[1:2] * stat[2:3]

    @tiles
    def _(c):
        at = lanes_of(c)
        d = (live() * (stat[6:7, at] * stat[1:2, at])
             * (fac[c] - stat[4:5, at] - conv[c] * stat[5:6, at])).astype(bf16)
        ds_[0, :, at] = d[:REACH]
        ds_[1, :, at] = d[ROWS - REACH:]
        dwide[c, pl.ds(REACH, ROWS), :] = d.astype(f32)

    halo_done = halo(ds_, dr_)

    u_done()
    u_all = summed(u2)
    k_done()
    u_rows, q_rows = u_all[0:4], u_all[4:8]
    inv = stat[1:2]
    k3[z] = (stat[6:7] * inv) * (
        summed(k2) - stat[4:5] * u_rows - stat[5:6] * (inv * (q_rows - stat[0:1] * u_rows)))
    k_done = exchange(k3, z, on_z)

    owner = 2 * x + yl
    gzb = rsems()
    slot = rem(z + 8 - owner, 8)

    def y_part(q):
        gy_done[q]()
        t = gyf[q, pl.ds(yl * 12 + yh * 3, 3)]
        for d in range(1, 8):
            t = t + gyr[q, d].astype(f32)
        gz[q] = t
        gzs[q] = t.astype(bf16)

    y_part(0)
    y_part(1)
    to_owner = copy(gzs, gzr.at[slot], gzb, on_z(owner))
    cond.append((z != owner, [to_owner]))

    @pl.when(z != owner)
    def _():
        to_owner.start()

    halo_done()
    x2_done = zy_part(2)

    @tiles
    def _(c):
        at = lanes_of(c)
        dwide[c, pl.ds(0, REACH), :] = dr_[0, :, at].astype(f32)
        dwide[c, pl.ds(REACH + ROWS, REACH), :] = dr_[1, :, at].astype(f32)
        acc = jnp.zeros((ROWS, LANES), f32)
        for k in range(TAPS):
            acc = acc + kern[pl.ds(k, 1), at] * dwide[c, pl.ds(TAPS - k, ROWS), :]
        v = glu[:, at].astype(f32)
        sg = jax.nn.sigmoid(glu[:, lanes_of(c, CH)].astype(f32))
        du = live() * acc * sg
        gg[:, at] = du.astype(bf16)
        gg[:, lanes_of(c, CH)] = (du * v * (1.0 - sg)).astype(bf16)

    store_gg = pltpu.make_async_copy(gg, gg_hbm, lsem.at[7])
    store_gg.start()

    k_done()
    kf[g] = summed(k3) * stat[3:4]
    k_done = exchange(kf, g, on_g)

    zyx_part(2, x2_done)

    fbb = rsems(2)
    spread = []
    for d in range(1, 16):
        e = rem(core + d, 2)
        c_ = rem(ctx + d // 2, 8)
        spread.append(copy(fin.at[pl.ds(e, 2)], fb.at[core], fbb + core, (div(dp, 2) * 2 + e, c_)))
    cond.append((z == owner, spread))

    @pl.when(z == owner)
    def _():
        arrived(gzr.at[pl.ds(1, 7)], gzb)
        for q in (0, 1):
            t = gz[q]
            for d in range(1, 8):
                t = t + gzr[d, q].astype(f32)
            t = t * stat[3:4, 0:LANES].reshape(1, 1, LANES)
            for u in range(3):
                fin[u, q] = t[u]
        for c in spread:
            c.start()
        fb[core] = fin[pl.ds(core, 2)]

    k_done()
    for j in range(8):
        w = 4 if j < 7 else 3
        gk_ref[pl.ds(4 * j, w), :] = kf[j, 0:w, :]

    @pl.when(z != owner)
    def _():
        arrived(fb.at[core], fbb + core)

    arrived(fb.at[sib], fbb + sib)
    arrived(hfb.at[sib, 2], h3 + 2)
    for h in range(2):
        for q in range(CHUNKS):
            v = jnp.concatenate([fb[h, 0, q], fb[h, 1, q]], 0) if q < 2 else hfb[h, q].reshape(16, LANES)
            gp_ref[:, pl.ds(h * HALF + q * LANES, LANES)] = jnp.where(core == 0, v[0:BLOCK], v[16 - BLOCK:16])

    finish()
    store_out.wait()
    store_gg.wait()


def handed_on(*refs):
    sem = refs[12]
    copies = [pltpu.make_async_copy(refs[i], refs[6 + i], sem.at[i]) for i in range(6)]
    for c in copies:
        c.start()
    for c in copies:
        c.wait()


def body(glu_in, lengths, kernel, bn_gain, bn_bias, proj_weight, cotangent):
    vm = pltpu.VMEM
    hbm = functools.partial(pltpu.with_memory_space_constraint, memory_space=pltpu.HBM)
    anyspec = pl.BlockSpec(memory_space=pl.ANY)
    vspec = pl.BlockSpec(memory_space=pltpu.VMEM)
    sspec = pl.BlockSpec(memory_space=pltpu.SMEM)
    scratch = [
        vm((ROWS, 2 * CH), bf16), vm((ROWS, CH), bf16), vm((TAPS, CH), f32),
        vm((TILES, ROWS + 2 * REACH, LANES), f32), vm((TILES, ROWS, LANES), f32),
        vm((TILES, ROWS, LANES), f32), vm((TILES, ROWS + 2 * REACH, LANES), f32),
        vm((ROWS, CH), f32), vm((ROWS, CH), bf16), vm((ROWS, CH), bf16), vm((ROWS, 2 * CH), bf16),
        vm((ROWS + 2 * REACH, CH), bf16),
        vm((BLOCK, CH), bf16), vm((NC, BLOCK, HALF), bf16),
        vm((NC, NYH, NZ, 3, 8, HALF), bf16), vm((NC, CH, HALF), bf16),
        vm((2, REACH, CH), bf16), vm((2, REACH, CH), bf16), vm((2, REACH, CH), bf16), vm((2, REACH, CH), bf16),
        vm((8, 2, CH + LANES), f32), vm((8, 2, CH + LANES), f32), vm((8, 2, CH + LANES), f32),
        vm((8, 2, CH), f32), vm((8, 2, CH), f32), vm((8, 2, CH), f32),
        vm((8, CH), f32),
        vm((8, 4, CH), f32), vm((8, 4, CH), f32), vm((8, 4, CH), f32), vm((8, 4, CH), f32), vm((8, 4, CH), f32),
        vm((8, 8, CH), f32), vm((8, 8, CH), f32), vm((8, 8, CH), f32),
        vm((CHUNKS, CH, LANES), f32), vm((CHUNKS, CH, LANES), bf16), vm((CHUNKS, CH, LANES), bf16),
        vm((2, NX, 192, LANES), bf16), vm((2, NX, 192, LANES), bf16),
        vm((2, 24, 8, LANES), f32), vm((2, 24, 8, LANES), bf16), vm((2, 8, 3, 8, LANES), bf16),
        vm((2, 3, 8, LANES), f32), vm((2, 3, 8, LANES), bf16), vm((8, 2, 3, 8, LANES), bf16),
        vm((3, 2, 8, LANES), f32), vm((2, 2, 2, 8, LANES), f32),
        vm((CHUNKS, NZ, 96, LANES), bf16), vm((CHUNKS, NZ, 96, LANES), bf16),
        vm((CHUNKS, 12, 8, LANES), bf16), vm((CHUNKS, 8, 3, 8, LANES), bf16),
        vm((CHUNKS, NX, 3, 8, LANES), f32), vm((CHUNKS, 3, 8, LANES), f32), vm((2, CHUNKS, 2, 8, LANES), f32),
        vm((CH,), f32), vm((CH,), f32),
        pltpu.SemaphoreType.DMA((56,)), pltpu.SemaphoreType.DMA((46,)), pltpu.SemaphoreType.DMA((8,)),
    ]
    outs = [
        jax.ShapeDtypeStruct((ROWS, CH), bf16),
        jax.ShapeDtypeStruct((ROWS, 2 * CH), bf16),
        jax.ShapeDtypeStruct((BLOCK, CH), f32),
        jax.ShapeDtypeStruct((TAPS, CH), f32),
        jax.ShapeDtypeStruct((CH,), f32),
        jax.ShapeDtypeStruct((CH,), f32),
    ]
    results = pl.pallas_call(
        fused,
        out_shape=outs,
        in_specs=[anyspec, sspec, anyspec, anyspec, anyspec, anyspec, anyspec],
        out_specs=[anyspec, anyspec, vspec, vspec, vspec, vspec],
        scratch_shapes=scratch,
        compiler_params=pltpu.CompilerParams(
            collective_id=0, has_side_effects=True, vmem_limit_bytes=40 * 1024 * 1024),
        name="conformer_conv",
    )(hbm(glu_in[0]), lengths, hbm(kernel), hbm(bn_gain), hbm(bn_bias), hbm(proj_weight), hbm(cotangent[0]))
    result, grad_glu, grad_proj, grad_kernel, grad_gain, grad_bias = pl.pallas_call(
        handed_on,
        out_shape=outs,
        in_specs=[anyspec] * 6,
        out_specs=[anyspec] * 6,
        scratch_shapes=[pltpu.SemaphoreType.DMA((6,))],
        compiler_params=pltpu.CompilerParams(vmem_limit_bytes=1024 * 1024),
        name="handed_on",
    )(*results)
    return (result[None], grad_glu[None], grad_proj, grad_kernel, grad_gain, grad_bias)


def solution(mesh):
    in_specs = (P("dp", "ctx", None), P("dp"), P(), P(), P(), P("dp", None), P("dp", "ctx", None))
    out_specs = (P("dp", "ctx", None), P("dp", "ctx", None), P("dp", None), P(), P(), P())
    return jax.shard_map(body, mesh=mesh, in_specs=in_specs, out_specs=out_specs, check_vma=False)
```

```python
import functools

import jax
import jax.numpy as jnp
from jax import lax
from jax.experimental import pallas as pl
from jax.experimental.pallas import tpu as pltpu
from jax.sharding import PartitionSpec as P

eps = 1e-05
f32 = jnp.float32
bf16 = jnp.bfloat16

NZ, NYH, NC, NYL, NX = 8, 4, 2, 2, 4
ROWS, CH, TAPS, LANES = 128, 768, 31, 128
TILES = CH // LANES
HALF = CH // 2
REACH = 16
BLOCK = CH // (NZ * NYH * NC)
CHUNKS = HALF // LANES
NEAR = (0, 1, 7, 2, 6, 3, 5, 4)


def rem(a, b):
    return lax.rem(a, jnp.int32(b))


def div(a, b):
    return lax.div(a, jnp.int32(b))


def lanes_of(c, first=0):
    return pl.ds(pl.multiple_of(first + c * LANES, LANES), LANES)


def farthest(n):
    return sorted(range(1, n), key=lambda d: -min(d, n - d))


def tiles(fn):
    def step(c, carry):
        fn(c)
        return carry

    lax.fori_loop(0, TILES, step, 0)


def fused(glu_hbm, len_ref, kern_hbm, gain_in, bias_in, w_hbm, cot_hbm,
          out_hbm, gg_hbm, gp_ref, gk_ref, gn_ref, gb_ref,
          glu, cot, kern, unit, conv, fac, dwide, da, act, out, gg, ub,
          wl, wr, wb, wfull, hs, hr, ds_, dr_, a1, a2, a3, b1, b2, b3, stat,
          kt, kr, k2, k3, kf, uq, ur, u2, gown, gsend, grc, gxs, gxr, gyf, gys, gyr, gz, gzs, gzr, fin, fb,
          hz, hzr, hy, hyr, hx, hfin, hfb,
          gain_v, bias_v, ssem, rsem, lsem):
    dp = lax.axis_index("dp")
    ctx = lax.axis_index("ctx")
    z, yh, core = div(dp, 8), rem(div(dp, 2), 4), rem(dp, 2)
    yl, x = div(ctx, 4), rem(ctx, 4)
    y = yh * 2 + yl
    g = x * 2 + core
    sib = 1 - core

    def dev(z_, y_, x_, c_):
        return (z_ * 8 + div(y_, 2) * 2 + c_, rem(y_, 2) * 4 + x_)

    def on_g(j):
        return dev(z, y, div(j, 2), rem(j, 2))

    def on_y(j):
        return dev(z, j, x, core)

    def on_z(j):
        return dev(j, y, x, core)

    def on_x(j):
        return dev(z, y, j, core)

    sibling = dev(z, y, x, sib)
    used = [0, 0]
    pending = []
    cond = []

    def ssems(n=1):
        used[0] += n
        return used[0] - n

    def rsems(n=1):
        used[1] += n
        return used[1] - n

    def desc(src, dst, ssend, recv, target):
        return pltpu.make_async_remote_copy(
            src_ref=src, dst_ref=dst, send_sem=ssem.at[ssend], recv_sem=rsem.at[recv],
            device_id=target, device_id_type=pl.DeviceIdType.MESH)

    def copy(src, dst, recv, target):
        return desc(src, dst, ssems(), recv, target)

    def send(src, dst, recv, target):
        c = copy(src, dst, recv, target)
        c.start()
        pending.append(c)

    def group(copies, total, recv):
        sem = ssems()
        for src, dst, target in copies:
            desc(src, dst, sem, recv, target).start()
        pending.append(desc(total, total, sem, recv, sibling))

    def arrived(dst, recv):
        desc(dst, dst, 0, recv, sibling).wait_recv()

    def finish():
        for c in pending:
            c.wait_send()
        for when, copies in cond:
            @pl.when(when)
            def _():
                for c in copies:
                    c.wait_send()

    def exchange(buf, me, where, n=8):
        recv = rsems()
        others = buf.at[pl.ds(0, n - 1)]
        group([(buf.at[me], buf.at[me], where(rem(me + d, n))) for d in farthest(n)], others, recv)
        return lambda: arrived(others, recv)

    def scatter(src_of, dst_of, total_src, total_dst, me, where, n=8):
        recv = rsems()
        copies = []
        for d in farthest(n):
            j = rem(me + d, n)
            copies.append((src_of(j), dst_of(d), where(j)))
        group(copies, total_src, recv)
        return lambda: arrived(total_dst, recv)

    barrier = pltpu.get_barrier_semaphore()
    peers = [on_g(rem(g + d, 8)) for d in range(1, 8)]
    peers += [on_y(rem(y + d, 8)) for d in range(1, 8)]
    peers += [on_z(rem(z + d, 8)) for d in range(1, 8)]
    flip = yh * 2 + (1 - yl)
    peers += [dev(z, rem(y + 2 * d, 8), x, sib) for d in range(1, 4)]
    peers += [dev(z, flip, div(rem(g + d, 8), 2), rem(rem(g + d, 8), 2)) for d in range(1, 8)]
    for p in peers:
        pl.semaphore_signal(barrier, inc=1, device_id=p, device_id_type=pl.DeviceIdType.MESH)

    loads = [pltpu.make_async_copy(a, b, lsem.at[i]) for i, (a, b) in enumerate(
        [(glu_hbm, glu), (kern_hbm, kern), (cot_hbm, cot), (gain_in, gain_v), (bias_in, bias_v)])]
    load_w = pltpu.make_async_copy(w_hbm, wl, lsem.at[5])

    @pl.when(yh == x)
    def _():
        load_w.start()

    for c in loads:
        c.start()

    pos0 = ctx * ROWS
    length = len_ref[0]
    n_live = jnp.clip(length - pos0, 0, ROWS).astype(f32)

    def live():
        return (lax.broadcasted_iota(jnp.int32, (ROWS, LANES), 0) + pos0 < length).astype(f32)

    pl.semaphore_wait(barrier, len(peers))

    own_cols = pl.ds(pl.multiple_of(core * HALF, LANES), HALF)
    sib_cols = pl.ds(pl.multiple_of(sib * HALF, LANES), HALF)
    w1, w2, w3, w4 = rsems(2), rsems(2), rsems(8), rsems(2)
    mine = wb.at[core, x, 0]
    groups = ((0, 5), (5, 3))
    w4_sems = []
    w1_sends = [copy(wl.at[:, sib_cols], wr.at[core], w1 + core, sibling)]
    for d in range(1, 4):
        y_ = rem(yh + d, 4) * 2 + yl
        w1_sends.append(copy(wl.at[:, own_cols], wr.at[core], w1 + core, dev(z, y_, x, core)))
        w1_sends.append(copy(wl.at[:, sib_cols], wr.at[core], w1 + core, dev(z, y_, x, sib)))
    cond.append((yh == x, w1_sends))

    @pl.when(yh == x)
    def _():
        load_w.wait()
        for c in w1_sends:
            c.start()
        wr[core] = wl[:, own_cols]

    def w1_done():
        @pl.when(yh != x)
        def _():
            arrived(wr.at[core], w1 + core)

        arrived(wr.at[sib], w1 + sib)
        rows = jnp.concatenate([wr[0].astype(f32), wr[1].astype(f32)], 0)
        wb[core, x, 0] = rows.reshape(3, 8, HALF).astype(bf16)
        for i, (first, size) in enumerate(groups):
            places = range(max(first, 1), first + size)
            group([(mine, wb.at[core, x, p], on_z(rem(z + 8 - NEAR[p], 8))) for p in places],
                  wb.at[core, x, pl.ds(places[0], len(places))], w2 + i)

    loads[0].wait()

    @tiles
    def _(c):
        v = glu[:, lanes_of(c)].astype(f32)
        sg = jax.nn.sigmoid(glu[:, lanes_of(c, CH)].astype(f32))
        u = (live() * v * sg).astype(bf16)
        hs[0, :, lanes_of(c)] = u[:REACH]
        hs[1, :, lanes_of(c)] = u[ROWS - REACH:]
        ub[pl.ds(REACH, ROWS), lanes_of(c)] = u
        unit[c, pl.ds(REACH, ROWS), :] = u.astype(f32)

    @pl.when(ctx == 0)
    def _():
        hr[0] = jnp.zeros((REACH, CH), bf16)
        dr_[0] = jnp.zeros((REACH, CH), bf16)

    @pl.when(ctx == 7)
    def _():
        hr[1] = jnp.zeros((REACH, CH), bf16)
        dr_[1] = jnp.zeros((REACH, CH), bf16)


    def halo(src, dst):
        base = rsems(2)
        to_left = copy(src.at[0], dst.at[1], base + 1, (dp, ctx - 1))
        to_right = copy(src.at[1], dst.at[0], base, (dp, ctx + 1))

        @pl.when(ctx > 0)
        def _():
            to_left.start()

        @pl.when(ctx < 7)
        def _():
            to_right.start()

        def done():
            @pl.when(ctx > 0)
            def _():
                arrived(dst.at[0], base)
                to_left.wait_send()

            @pl.when(ctx < 7)
            def _():
                arrived(dst.at[1], base + 1)
                to_right.wait_send()

        return done

    halo_done = halo(hs, hr)

    halo_done()
    for c in (loads[1], loads[3], loads[4]):
        c.wait()
    stat[6:7] = gain_v[...].reshape(1, CH)
    stat[7:8] = bias_v[...].reshape(1, CH)
    ub[pl.ds(0, REACH), :] = hr[0]
    ub[pl.ds(REACH + ROWS, REACH), :] = hr[1]

    @tiles
    def _(c):
        unit[c, pl.ds(0, REACH), :] = hr[0, :, lanes_of(c)].astype(f32)
        unit[c, pl.ds(REACH + ROWS, REACH), :] = hr[1, :, lanes_of(c)].astype(f32)
        acc = jnp.zeros((ROWS, LANES), f32)
        for k in range(TAPS):
            acc = acc + kern[pl.ds(k, 1), lanes_of(c)] * unit[c, pl.ds(k + 1, ROWS), :]
        conv[c] = acc
        m = live()
        s = jnp.sum(m * acc, 0, keepdims=True)
        centred = acc - s / jnp.maximum(n_live, 1.0)
        q = jnp.sum(m * centred * centred, 0, keepdims=True)
        a1[g, :, lanes_of(c)] = jnp.concatenate([s, q], 0)

    a1[g, :, pl.ds(CH, LANES)] = jnp.full((2, LANES), n_live, f32)

    def merged(buf):
        total = buf[0]
        for i in range(1, 8):
            total = total + buf[i]
        s, q, n = total[0:1, 0:CH], total[1:2, 0:CH], total[0:1, CH:]
        mean = s / jnp.maximum(jnp.concatenate([n] * TILES, 1), 1.0)
        for i in range(8):
            n_i = buf[i, 0:1, CH:]
            r_i = 1.0 / jnp.maximum(n_i, 1.0)
            off = buf[i, 0:1, 0:CH] - jnp.concatenate([n_i] * TILES, 1) * mean
            q = q + off * off * jnp.concatenate([r_i] * TILES, 1)
        return s, q, n

    def packed(s, q, n):
        return jnp.concatenate([jnp.concatenate([s, n], 1), jnp.concatenate([q, n], 1)], 0)

    def summed(buf):
        total = buf[0]
        for i in range(1, 8):
            total = total + buf[i]
        return total

    a_done = exchange(a1, g, on_g)

    w1_done()

    n_rows = jnp.clip(length - pos0, 0, ROWS)
    tap = lax.broadcasted_iota(jnp.int32, (32, ROWS + 2 * REACH), 0)
    row = lax.broadcasted_iota(jnp.int32, (32, ROWS + 2 * REACH), 1) - tap - 1
    window = ((row >= 0) & (row < n_rows) & (tap < TAPS)).astype(f32).astype(bf16)
    u_sum = jnp.dot(window, ub[...], preferred_element_type=f32)
    for j in range(8):
        uq[j, 0:4, :] = u_sum[4 * j:4 * j + 4]

    @tiles
    def _(c):
        at = lanes_of(c)
        d = live() * conv[c]
        for k in range(TAPS):
            uq[k // 4, pl.ds(4 + k % 4, 1), at] = jnp.sum(d * unit[c, pl.ds(k + 1, ROWS), :], 0, keepdims=True)
        uq[7, 7:8, at] = jnp.zeros((1, LANES), f32)

    a_done()
    a2[y] = packed(*merged(a1))
    a_done = exchange(a2, y, on_y)

    def onward(i):
        first, size = groups[i]
        some = max(first, 1)
        arrived(wb.at[core, x, pl.ds(some, first + size - some)], w2 + i)
        strip = wb.at[core, x, pl.ds(first, size)]
        sem = ssems()
        for d in range(1, 4):
            desc(strip, strip, sem, w3 + 4 * i + d, on_x(rem(x + d, 4))).start()
        pending.append(desc(wb.at[core, pl.ds(0, 3), pl.ds(first, size)],
                            wb.at[core, pl.ds(0, 3), pl.ds(first, size)], sem, 0, sibling))
        w4_sems.append(ssems())
        desc(strip, strip, w4_sems[i], w4 + i, sibling).start()

    def across(i):
        first, size = groups[i]
        for d in range(1, 4):
            piece = wb.at[core, rem(x + (4 - d), 4), pl.ds(first, size)]
            arrived(piece, w3 + 4 * i + d)
            desc(piece, piece, w4_sems[i], w4 + i, sibling).start()
        whole = wb.at[core, :, pl.ds(first, size)]
        pending.append(desc(whole, whole, w4_sems[i], 0, sibling))

    onward(0)
    onward(1)
    a_done()
    a3[z] = packed(*merged(a2))
    a_done = exchange(a3, z, on_z)
    uq_done = scatter(lambda j: uq.at[j], lambda d: ur.at[d], uq.at[pl.ds(0, 7)], ur.at[pl.ds(1, 7)], g, on_g)
    across(0)
    a_done()
    s, q, n = merged(a3)
    n = jnp.concatenate([n] * TILES, 1)
    stat[0:1] = s / n
    stat[1:2] = lax.rsqrt(q / n + eps)
    stat[2:3] = 1.0 / n
    stat[3:4] = lax.rsqrt(n)

    @tiles
    def _(c):
        at = lanes_of(c)
        normed = (conv[c] - stat[0:1, at]) * stat[1:2, at]
        conv[c] = normed
        pre = stat[6:7, at] * normed + stat[7:8, at]
        sp = jax.nn.sigmoid(pre)
        m = live()
        act[:, at] = (m * pre * sp).astype(bf16)
        fac[c] = m * sp * (1.0 + pre * (1.0 - sp))

    across(1)
    for i, (first, size) in enumerate(groups):
        arrived(wb.at[sib, :, pl.ds(first, size)], w4 + i)
    for p in range(NZ):
        rows = pl.ds(pl.multiple_of(rem(z + NEAR[p], 8) * 96, 16), 96)
        for h in range(2):
            wfull[h, rows, :] = wb[h, :, p].astype(f32).reshape(96, HALF).astype(bf16)
    uq_done()
    t = uq[g]
    for d in range(1, 8):
        t = t + ur[d]
    u2[y] = t
    u_done = exchange(u2, y, on_y)
    loads[2].wait()
    nt = (((1,), (1,)), ((), ()))
    da[...] = (lax.dot_general(cot[:, 0:HALF], wfull[0], nt, preferred_element_type=f32)
               + lax.dot_general(cot[:, HALF:CH], wfull[1], nt, preferred_element_type=f32))

    @tiles
    def _(c):
        at = lanes_of(c)
        d_pre = da[:, at] * fac[c]
        fac[c] = d_pre
        b1[g, :, at] = jnp.concatenate(
            [jnp.sum(d_pre, 0, keepdims=True), jnp.sum(d_pre * conv[c], 0, keepdims=True)], 0)

    b_done = exchange(b1, g, on_g)

    tn = (((0,), (0,)), ((), ()))

    gc, h3 = rsems(CHUNKS), rsems(CHUNKS)
    h1_done, h2_done = {}, {}

    @tiles
    def _(c):
        at = lanes_of(c)
        rows = pl.ds(pl.multiple_of(c * LANES, LANES), LANES)
        a = act[:, at]
        g_sib = lax.dot_general(a, cot[:, sib_cols], tn, preferred_element_type=f32).astype(bf16)
        g_own = lax.dot_general(a, cot[:, own_cols], tn, preferred_element_type=f32)
        for q in range(CHUNKS):
            gsend[q, rows, :] = g_sib[:, q * LANES:(q + 1) * LANES]
            gown[q, rows, :] = g_own[:, q * LANES:(q + 1) * LANES]
        d = fac[c]
        for k in range(TAPS):
            kt[k // 4, pl.ds(k % 4, 1), at] = jnp.sum(d * unit[c, pl.ds(k + 1, ROWS), :], 0, keepdims=True)
        kt[7, 3:4, at] = jnp.zeros((1, LANES), f32)

    for q in range(CHUNKS):
        send(gsend.at[q], grc.at[q], gc + q, sibling)
    k1_done = scatter(lambda j: kt.at[j], lambda d: kr.at[d], kt.at[pl.ds(0, 7)], kr.at[pl.ds(1, 7)], g, on_g)
    gx_done = []

    def x_send(q):
        return scatter(lambda j: gxs.at[q, j], lambda d: gxr.at[q, d],
                       gxs.at[q, pl.ds(0, 3)], gxr.at[q, pl.ds(1, 3)], x, on_x, NX)

    for q in (0, 1):
        arrived(grc.at[q], gc + q)
        t = gown[q] + grc[q].astype(f32)
        gown[q] = t
        gxs[q] = t.astype(bf16).reshape(NX, 192, LANES)
        gx_done.append(x_send(q))

    b_done()
    b2[z] = summed(b1)
    b_done = exchange(b2, z, on_z)

    arrived(grc.at[2], gc + 2)
    t = gown[2] + grc[2].astype(f32)
    gown[2] = t
    hz[2] = t.astype(bf16).reshape(NZ, 96, LANES)
    h1_done[2] = scatter(lambda j: hz.at[2, j], lambda d: hzr.at[2, d],
                         hz.at[2, pl.ds(0, 7)], hzr.at[2, pl.ds(1, 7)], z, on_z)

    k1_done()
    t = kt[g]
    for d in range(1, 8):
        t = t + kr[d]
    k2[y] = t
    k_done = exchange(k2, y, on_y)
    b_done()
    b3[y] = summed(b2)
    b_done = exchange(b3, y, on_y)

    def x_part(q):
        gx_done[q]()
        t = gown[q, pl.ds(pl.multiple_of(x * 192, 16), 192), :]
        for d in range(1, 4):
            t = t + gxr[q, d].astype(f32)
        t = t.reshape(24, 8, LANES)
        gyf[q] = t
        gys[q] = t.astype(bf16)
        return scatter(lambda j: gys.at[q, pl.ds(rem(j, 2) * 12 + div(j, 2) * 3, 3)], lambda d: gyr.at[q, d],
                       gyr.at[q, pl.ds(0, 7)], gyr.at[q, pl.ds(1, 7)], y, on_y)

    def z_part(q):
        h1_done[q]()
        t = gown[q, pl.ds(pl.multiple_of(z * 96, 16), 96), :]
        for d in range(1, 8):
            t = t + hzr[q, d].astype(f32)
        hy[q] = t.reshape(12, 8, LANES).astype(bf16)
        h2_done[q] = scatter(lambda j: hy.at[q, pl.ds(div(j, 2) * 3, 3)], lambda d: hyr.at[q, y],
                             hyr.at[q, pl.ds(0, 7)], hyr.at[q, pl.ds(0, 7)], y, on_y)
        hyr[q, y] = hy[q, pl.ds(yh * 3, 3)]

    def zy_part(q):
        h2_done[q]()
        t = hyr[q, 0].astype(f32)
        for i in range(1, 8):
            t = t + hyr[q, i].astype(f32)
        hx[q, x] = t
        return exchange(hx.at[q], x, on_x, NX)

    def zyx_part(q, done):
        done()
        t = hx[q, 0]
        for i in range(1, NX):
            t = t + hx[q, i]
        hfin[q] = t * stat[3:4, 0:LANES].reshape(1, 1, LANES)
        send(hfin.at[q, pl.ds(sib, 2)], hfb.at[core, q], h3 + q, sibling)
        hfb[core, q] = hfin[q, pl.ds(core, 2)]

    gy_done = [x_part(0), x_part(1)]
    for h in range(2):
        out[:, h * HALF:(h + 1) * HALF] = jnp.dot(act[...], wfull[h], preferred_element_type=f32).astype(bf16)
    store_out = pltpu.make_async_copy(out, out_hbm, lsem.at[6])
    store_out.start()
    z_part(2)
    b_done()
    sums = summed(b3)
    gb_ref[...] = (sums[0:1] * stat[3:4]).reshape(CH)
    gn_ref[...] = (sums[1:2] * stat[3:4]).reshape(CH)
    stat[4:5] = sums[0:1] * stat[2:3]
    stat[5:6] = sums[1:2] * stat[2:3]

    @tiles
    def _(c):
        at = lanes_of(c)
        d = (live() * (stat[6:7, at] * stat[1:2, at])
             * (fac[c] - stat[4:5, at] - conv[c] * stat[5:6, at])).astype(bf16)
        ds_[0, :, at] = d[:REACH]
        ds_[1, :, at] = d[ROWS - REACH:]
        dwide[c, pl.ds(REACH, ROWS), :] = d.astype(f32)

    halo_done = halo(ds_, dr_)

    u_done()
    u_all = summed(u2)
    k_done()
    u_rows, q_rows = u_all[0:4], u_all[4:8]
    inv = stat[1:2]
    k3[z] = (stat[6:7] * inv) * (
        summed(k2) - stat[4:5] * u_rows - stat[5:6] * (inv * (q_rows - stat[0:1] * u_rows)))
    k_done = exchange(k3, z, on_z)

    owner = 2 * x + yl
    gzb = rsems()
    slot = rem(z + 8 - owner, 8)

    def y_part(q):
        gy_done[q]()
        t = gyf[q, pl.ds(yl * 12 + yh * 3, 3)]
        for d in range(1, 8):
            t = t + gyr[q, d].astype(f32)
        gz[q] = t
        gzs[q] = t.astype(bf16)

    y_part(0)
    y_part(1)
    to_owner = copy(gzs, gzr.at[slot], gzb, on_z(owner))
    cond.append((z != owner, [to_owner]))

    @pl.when(z != owner)
    def _():
        to_owner.start()

    halo_done()
    x2_done = zy_part(2)

    @tiles
    def _(c):
        at = lanes_of(c)
        dwide[c, pl.ds(0, REACH), :] = dr_[0, :, at].astype(f32)
        dwide[c, pl.ds(REACH + ROWS, REACH), :] = dr_[1, :, at].astype(f32)
        acc = jnp.zeros((ROWS, LANES), f32)
        for k in range(TAPS):
            acc = acc + kern[pl.ds(k, 1), at] * dwide[c, pl.ds(TAPS - k, ROWS), :]
        v = glu[:, at].astype(f32)
        sg = jax.nn.sigmoid(glu[:, lanes_of(c, CH)].astype(f32))
        du = live() * acc * sg
        gg[:, at] = du.astype(bf16)
        gg[:, lanes_of(c, CH)] = (du * v * (1.0 - sg)).astype(bf16)

    store_gg = pltpu.make_async_copy(gg, gg_hbm, lsem.at[7])
    store_gg.start()

    k_done()
    kf[g] = summed(k3) * stat[3:4]
    k_done = exchange(kf, g, on_g)

    zyx_part(2, x2_done)

    fbb = rsems(2)
    spread = []
    for d in range(1, 16):
        e = rem(core + d, 2)
        c_ = rem(ctx + d // 2, 8)
        spread.append(copy(fin.at[pl.ds(e, 2)], fb.at[core], fbb + core, (div(dp, 2) * 2 + e, c_)))
    cond.append((z == owner, spread))

    @pl.when(z == owner)
    def _():
        arrived(gzr.at[pl.ds(1, 7)], gzb)
        for q in (0, 1):
            t = gz[q]
            for d in range(1, 8):
                t = t + gzr[d, q].astype(f32)
            t = t * stat[3:4, 0:LANES].reshape(1, 1, LANES)
            for u in range(3):
                fin[u, q] = t[u]
        for c in spread:
            c.start()
        fb[core] = fin[pl.ds(core, 2)]

    k_done()
    for j in range(8):
        w = 4 if j < 7 else 3
        gk_ref[pl.ds(4 * j, w), :] = kf[j, 0:w, :]

    @pl.when(z != owner)
    def _():
        arrived(fb.at[core], fbb + core)

    arrived(fb.at[sib], fbb + sib)
    arrived(hfb.at[sib, 2], h3 + 2)
    for h in range(2):
        for q in range(CHUNKS):
            v = jnp.concatenate([fb[h, 0, q], fb[h, 1, q]], 0) if q < 2 else hfb[h, q].reshape(16, LANES)
            gp_ref[:, pl.ds(h * HALF + q * LANES, LANES)] = jnp.where(core == 0, v[0:BLOCK], v[16 - BLOCK:16])

    finish()
    store_out.wait()
    store_gg.wait()


def handed_on(*refs):
    sem = refs[12]
    copies = [pltpu.make_async_copy(refs[i], refs[6 + i], sem.at[i]) for i in range(6)]
    for c in copies:
        c.start()
    for c in copies:
        c.wait()


def body(glu_in, lengths, kernel, bn_gain, bn_bias, proj_weight, cotangent):
    vm = pltpu.VMEM
    hbm = functools.partial(pltpu.with_memory_space_constraint, memory_space=pltpu.HBM)
    anyspec = pl.BlockSpec(memory_space=pl.ANY)
    vspec = pl.BlockSpec(memory_space=pltpu.VMEM)
    sspec = pl.BlockSpec(memory_space=pltpu.SMEM)
    scratch = [
        vm((ROWS, 2 * CH), bf16), vm((ROWS, CH), bf16), vm((TAPS, CH), f32),
        vm((TILES, ROWS + 2 * REACH, LANES), f32), vm((TILES, ROWS, LANES), f32),
        vm((TILES, ROWS, LANES), f32), vm((TILES, ROWS + 2 * REACH, LANES), f32),
        vm((ROWS, CH), f32), vm((ROWS, CH), bf16), vm((ROWS, CH), bf16), vm((ROWS, 2 * CH), bf16),
        vm((ROWS + 2 * REACH, CH), bf16),
        vm((BLOCK, CH), bf16), vm((NC, BLOCK, HALF), bf16),
        vm((NC, NYH, NZ, 3, 8, HALF), bf16), vm((NC, CH, HALF), bf16),
        vm((2, REACH, CH), bf16), vm((2, REACH, CH), bf16), vm((2, REACH, CH), bf16), vm((2, REACH, CH), bf16),
        vm((8, 2, CH + LANES), f32), vm((8, 2, CH + LANES), f32), vm((8, 2, CH + LANES), f32),
        vm((8, 2, CH), f32), vm((8, 2, CH), f32), vm((8, 2, CH), f32),
        vm((8, CH), f32),
        vm((8, 4, CH), f32), vm((8, 4, CH), f32), vm((8, 4, CH), f32), vm((8, 4, CH), f32), vm((8, 4, CH), f32),
        vm((8, 8, CH), f32), vm((8, 8, CH), f32), vm((8, 8, CH), f32),
        vm((CHUNKS, CH, LANES), f32), vm((CHUNKS, CH, LANES), bf16), vm((CHUNKS, CH, LANES), bf16),
        vm((2, NX, 192, LANES), bf16), vm((2, NX, 192, LANES), bf16),
        vm((2, 24, 8, LANES), f32), vm((2, 24, 8, LANES), bf16), vm((2, 8, 3, 8, LANES), bf16),
        vm((2, 3, 8, LANES), f32), vm((2, 3, 8, LANES), bf16), vm((8, 2, 3, 8, LANES), bf16),
        vm((3, 2, 8, LANES), f32), vm((2, 2, 2, 8, LANES), f32),
        vm((CHUNKS, NZ, 96, LANES), bf16), vm((CHUNKS, NZ, 96, LANES), bf16),
        vm((CHUNKS, 12, 8, LANES), bf16), vm((CHUNKS, 8, 3, 8, LANES), bf16),
        vm((CHUNKS, NX, 3, 8, LANES), f32), vm((CHUNKS, 3, 8, LANES), f32), vm((2, CHUNKS, 2, 8, LANES), f32),
        vm((CH,), f32), vm((CH,), f32),
        pltpu.SemaphoreType.DMA((56,)), pltpu.SemaphoreType.DMA((46,)), pltpu.SemaphoreType.DMA((8,)),
    ]
    outs = [
        jax.ShapeDtypeStruct((ROWS, CH), bf16),
        jax.ShapeDtypeStruct((ROWS, 2 * CH), bf16),
        jax.ShapeDtypeStruct((BLOCK, CH), f32),
        jax.ShapeDtypeStruct((TAPS, CH), f32),
        jax.ShapeDtypeStruct((CH,), f32),
        jax.ShapeDtypeStruct((CH,), f32),
    ]
    results = pl.pallas_call(
        fused,
        out_shape=outs,
        in_specs=[anyspec, sspec, anyspec, anyspec, anyspec, anyspec, anyspec],
        out_specs=[anyspec, anyspec, vspec, vspec, vspec, vspec],
        scratch_shapes=scratch,
        compiler_params=pltpu.CompilerParams(
            collective_id=0, has_side_effects=True, vmem_limit_bytes=40 * 1024 * 1024),
        name="conformer_conv",
    )(hbm(glu_in[0]), lengths, hbm(kernel), hbm(bn_gain), hbm(bn_bias), hbm(proj_weight), hbm(cotangent[0]))
    result, grad_glu, grad_proj, grad_kernel, grad_gain, grad_bias = pl.pallas_call(
        handed_on,
        out_shape=outs,
        in_specs=[anyspec] * 6,
        out_specs=[anyspec] * 6,
        scratch_shapes=[pltpu.SemaphoreType.DMA((6,))],
        compiler_params=pltpu.CompilerParams(vmem_limit_bytes=1024 * 1024),
        name="handed_on",
    )(*results)
    return (result[None], grad_glu[None], grad_proj, grad_kernel, grad_gain, grad_bias)


def solution(mesh):
    in_specs = (P("dp", "ctx", None), P("dp"), P(), P(), P(), P("dp", None), P("dp", "ctx", None))
    out_specs = (P("dp", "ctx", None), P("dp", "ctx", None), P("dp", None), P(), P(), P())
    return jax.shard_map(body, mesh=mesh, in_specs=in_specs, out_specs=out_specs, check_vma=False)
```
